32 devices in a mesh: mic: 8 (over z, x), orient: 4 (over y, core).
Axes of the slice: x: 2, y: 2, z: 4, core: 2. Of those that a mesh axis runs over, the one named last changes fastest.
Arguments:
- micrograph: bfloat16 [3072, 384], P('mic'), may hold values from -6 to 6
- search_spectra: bfloat16 [64, 384, 768], P('orient', 'mic'), may hold values from -6 to 6
- refine_spectra: bfloat16 [8, 32, 384, 768], P('mic', 'orient'), may hold values from -6 to 6
- ctf: float32 [384, 384], replicated, may hold values from -1 to 1
- ref_owner: int32 [128, 1], P(('mic', 'orient')), may hold values from 0 to 3; in each aligned block of 4 rows (0 to 3, 4 to 7, ...) at most 2 rows name the same one
- ref_slot: int32 [128, 1], P(('mic', 'orient')), may hold values from 0 to 7
Outputs:
- peak_map: float32 [3072, 384], P('mic')
- mean_map: float32 [3072, 384], P('mic')
- scaled_peak: float32 [3072, 384], P('mic')
- refined_map: float32 [3072, 384], P('mic')
The draws below stay inside these ranges and needn't reach their ends.
Inputs may be any that keep to these rules, and one draw needn't show every extreme that they name: `ref_owner`: in each aligned block of 4 rows (the list entries of one micrograph that one orientation block handles) no owner is named more than 2 times, and in some blocks one owner is named exactly 2 times.
All inputs are finite; a program needn't handle non-finite values.
Results may differ from the reference program's by a relative error of at most 0.0086.
Values may be sent and summed in bfloat16 or wider, within the bound.
A program may use at most 128 MiB of HBM per device.

```python
import math
import jax
import jax.numpy as jnp
import numpy as np
from jax import lax

P_SIZE = 384
RB = 8
RD = 4
CAP = 2
MICS = 8
NS = 64
RSET = 32
RL = 16
N_ORIENT = 4


def with_ends(drawn, own_key, low, high):
    longest = drawn.shape.index(max(drawn.shape))
    spots = []
    for shift in (0, 1):
        where = [jax.random.randint(jax.random.fold_in(own_key, axis), (), 0, length) for axis, length in enumerate(drawn.shape)]
        where[longest] = (where[longest] + shift) % drawn.shape[longest]
        spots.append(tuple(where))
    return drawn.at[spots[0]].set(low).at[spots[1]].set(high)


def block_scale(key, extent, cuts, smallest, high):
    gain = 1.0
    for dim, blocks in cuts:
        heights = jax.random.uniform(jax.random.fold_in(jax.random.fold_in(key, 6), dim), (blocks,), jnp.float32, smallest / len(cuts), high / len(cuts))
        gain = gain * jnp.repeat(jnp.exp(heights), extent[dim] // blocks).reshape((-1,) + (1,) * (len(extent) - 1 - dim))
    return gain


def shared_out(key, own, number, rows, amount, top, bound, lean):
    ranking = jax.random.permutation(key, amount)
    packed, usual = shares(amount, rows * top, bound, lean, True), shares(amount, rows * top, bound, lean, False)
    places = jnp.arange(amount)

    def named(tallies, rotation):
        used = int((tallies > 0).sum())
        fixed = max(1, used // 4)
        shifted = fixed + (places - fixed + rotation * (used - fixed)) % max(1, amount - fixed)
        return jnp.zeros((amount,), jnp.int32).at[ranking[jnp.where(places < fixed, places, shifted)]].set(jnp.asarray(tallies, jnp.int32))

    tallies = jnp.where(number % 4 == 0, named(packed, number // 4), named(usual, number - number // 4 - 1))
    mixed = jax.random.permutation(jax.random.fold_in(own, 3), amount)
    giver, receiver = mixed[0:amount // 2 * 2:2], mixed[1:amount // 2 * 2:2]
    margin = jnp.minimum(tallies[giver] - 1, bound - tallies[receiver]) // 2
    margin = jnp.where((giver == ranking[0]) | (receiver == ranking[0]) | (tallies[receiver] == 0), 0, jnp.maximum(margin, 0))
    shifted = jax.random.randint(jax.random.fold_in(own, 4), (amount // 2,), 0, 1 << 20) % (margin + 1)
    tallies = tallies.at[giver].add(-shifted).at[receiver].add(shifted)
    items = jnp.searchsorted(jnp.cumsum(tallies), jnp.arange(rows * top), side="right").astype(jnp.int32)
    table = items.reshape(top, rows).T
    table = table[jax.random.permutation(jax.random.fold_in(own, 1), rows)]
    rotation = jax.random.randint(jax.random.fold_in(own, 2), (rows, 1), 0, top)
    return jnp.take_along_axis(table, (jnp.arange(top)[None, :] + rotation) % top, axis=1)


def shares(number_of, total, most, slope, full):
    weights = [(1 << 20) // math.isqrt(grade ** slope) + 1 for grade in range(1, number_of + 1)]
    largest = most if full else min(most, max(-(-total // number_of), total * weights[0] // sum(weights)))
    least = 1 if total - largest >= number_of - 1 else 0
    counts, rest = [largest] + [least] * (number_of - 1), total - largest - least * (number_of - 1)
    while rest > 0:
        candidates = [i for i in range(1, number_of) if counts[i] < largest] or [i for i in range(1, number_of) if counts[i] < most]
        mass, budget = sum([weights[i] for i in candidates]), rest
        for i in candidates:
            more = min(most - counts[i], max(1, budget * weights[i] // mass), rest)
            counts[i] = counts[i] + more
            rest = rest - more
    return np.array(counts)


def normal_values(key, extent, width, most, split=(), kind=jnp.bfloat16):
    values = jax.random.normal(key, extent, jnp.float32) * width
    if len(split) > 0:
        values = block_scale(key, extent, split, -0.22, 0.18) * values
    return jnp.clip(values, min=-most, max=most).astype(kind)


def setup_inputs(seed: int = 0) -> dict:
    key_of = jax.random.split(jax.random.key(seed), 7)
    micrograph = normal_values(key_of[0], (MICS * P_SIZE, P_SIZE), 1.0, 6.0, ((0, 8),))
    search_spectra = normal_values(key_of[1], (NS, P_SIZE, 2 * P_SIZE), 1.0, 6.0, ((0, 4), (1, 8)))
    refine_spectra = normal_values(key_of[2], (MICS, RSET, P_SIZE, 2 * P_SIZE), 1.0, 6.0, ((0, 8), (1, 4)))
    ctf = jnp.clip(jax.random.uniform(key_of[3], (P_SIZE, P_SIZE), jnp.float32, -1.0, 1.0), -1.0, 1.0)
    ref_owner_keys = jax.random.split(jax.random.fold_in(key_of[4], 1), (MICS * RL) // RD)
    ref_owner_turns = jax.random.permutation(jax.random.fold_in(key_of[4], 3), (MICS * RL) // RD)
    ref_owner = jax.vmap(lambda own, number: shared_out(jax.random.fold_in(key_of[4], 2), own, number, RD, N_ORIENT, 1, CAP, 2))(ref_owner_keys, ref_owner_turns).reshape((MICS * RL, 1))
    ref_slot = with_ends(jax.random.randint(key_of[5], (MICS * RL, 1), 0, RB), jax.random.fold_in(key_of[5], 1), 0, RB - 1).astype(jnp.int32)
    return dict(micrograph=micrograph, search_spectra=search_spectra, refine_spectra=refine_spectra, ctf=ctf, ref_owner=ref_owner, ref_slot=ref_slot)


def make_tables(box_edge):
    positions = jnp.arange(box_edge, dtype=jnp.int32)
    products = positions[:, None] * positions[None, :] % box_edge
    angles = products.astype(jnp.float32) * (2.0 * math.pi / box_edge)
    cosine = jnp.cos(angles)
    sines = jnp.sin(angles)
    fwd_cos = cosine.astype(jnp.bfloat16)
    fwd_sin = sines.astype(jnp.bfloat16)
    inv_cos = (cosine / box_edge).astype(jnp.bfloat16)
    inv_sin = (sines / box_edge).astype(jnp.bfloat16)
    fwd_half = jnp.concatenate([fwd_cos, -fwd_sin], axis=1)
    fwd_full = jnp.stack([jnp.stack([fwd_cos, fwd_sin], -1), jnp.stack([-fwd_sin, fwd_cos], -1)], 0)
    inv_cols = jnp.concatenate([jnp.concatenate([inv_cos, inv_sin], 1), jnp.concatenate([-inv_sin, inv_cos], 1)], 0)
    inv_rows = jnp.stack([inv_cos, -inv_sin], -1)
    return (fwd_half, fwd_full, inv_cols, inv_rows)

def forward(tile_image, fwd_half, fwd_full):
    box_edge = tile_image.shape[0]
    half_spectrum = jnp.dot(tile_image, fwd_half, preferred_element_type=jnp.float32).astype(jnp.bfloat16)
    stacked = half_spectrum.reshape(box_edge, 2, box_edge)
    spectrum = jnp.einsum('dykc,kcx->ydx', fwd_full.astype(jnp.float32), stacked.astype(jnp.float32))
    return spectrum.reshape(box_edge, 2 * box_edge).astype(jnp.bfloat16)

def multiply(spectrum, filtered):
    box_edge = spectrum.shape[-1] // 2
    spec_real = spectrum[..., :box_edge].astype(jnp.float32)
    spec_imag = spectrum[..., box_edge:].astype(jnp.float32)
    filt_real = filtered[..., :box_edge].astype(jnp.float32)
    filt_imag = filtered[..., box_edge:].astype(jnp.float32)
    prod_real = spec_real * filt_real + spec_imag * filt_imag
    prod_imag = spec_imag * filt_real - spec_real * filt_imag
    return jnp.concatenate([prod_real, prod_imag], -1).astype(jnp.bfloat16)

def correlate(spectrum, filtered, inv_cols, inv_rows):
    box_edge = spectrum.shape[0]
    product = multiply(spectrum, filtered)
    halfway = jnp.einsum('trl,lm->trm', product.astype(jnp.float32), inv_cols.astype(jnp.float32)).astype(jnp.bfloat16)
    stacked = halfway.reshape(halfway.shape[0], box_edge, 2, box_edge)
    return jnp.einsum('ykc,tkcx->tyx', inv_rows.astype(jnp.float32), stacked.astype(jnp.float32))

def reference(micrograph, search_spectra, refine_spectra, ctf, ref_owner, ref_slot):
    box_edge = micrograph.shape[1]
    fwd_half, fwd_full, inv_cols, inv_rows = make_tables(box_edge)
    ctf_gain = jnp.concatenate([ctf, ctf], 1)
    search_filtered = (search_spectra.astype(jnp.float32) * ctf_gain).astype(jnp.bfloat16)
    tiles = micrograph.reshape(MICS, box_edge, box_edge)
    chosen_ids = (ref_owner[:, 0] * RB + ref_slot[:, 0]).astype(jnp.int32).reshape(MICS, RL)

    def one_tile(bundle):
        tile_image, library, chosen = bundle
        spectrum = forward(tile_image, fwd_half, fwd_full)
        correlations = correlate(spectrum, search_filtered, inv_cols, inv_rows)
        picked = jnp.take(library, chosen, axis=0)
        picked_filtered = (picked.astype(jnp.float32) * ctf_gain).astype(jnp.bfloat16)
        refined = lax.optimization_barrier(jnp.max(correlate(spectrum, picked_filtered, inv_cols, inv_rows), axis=0))
        return (lax.optimization_barrier(jnp.max(correlations, axis=0)), lax.optimization_barrier(jnp.sum(correlations, axis=0)), lax.optimization_barrier(jnp.sum(correlations * correlations, axis=0)), refined)
    peak_all, total_all, square_all, refined_all = lax.map(one_tile, (tiles, refine_spectra, chosen_ids))
    count = float(NS)
    peak_map = peak_all.reshape(MICS * box_edge, box_edge)
    mean_map = (total_all / count).reshape(MICS * box_edge, box_edge)
    scaled_peak = (peak_all * lax.rsqrt(square_all / count + 1e-05)).reshape(MICS * box_edge, box_edge)
    refined_map = refined_all.reshape(MICS * box_edge, box_edge)
    return (peak_map, mean_map, scaled_peak, refined_map)
```

```python
import functools
import math

import jax
import jax.numpy as jnp
import numpy as np
from jax import lax
from jax.experimental import pallas as pl
from jax.experimental.pallas import tpu as pltpu
from jax.sharding import PartitionSpec as P

MESH = pl.DeviceIdType.MESH
LOW = -3.0e38


def make_tables(box_edge):
    positions = np.arange(box_edge, dtype=np.int32)
    products = positions[:, None] * positions[None, :] % box_edge
    angles = products.astype(np.float32) * np.float32(2.0 * math.pi / box_edge)
    cosine = np.cos(angles)
    sines = np.sin(angles)
    narrow = lambda a: a.astype(np.float32).astype(jnp.bfloat16)
    fwd_cos, fwd_sin = narrow(cosine), narrow(sines)
    inv_cos = narrow(cosine / np.float32(box_edge))
    inv_sin = narrow(sines / np.float32(box_edge))
    return (fwd_cos, fwd_sin, inv_cos, inv_sin)


def forward(tile_image, fwd_cos, fwd_sin):
    box_edge = tile_image.shape[0]
    full_map = jnp.asarray(np.concatenate([fwd_cos, fwd_sin], 1))
    halved = jnp.dot(tile_image, full_map, preferred_element_type=jnp.float32).astype(jnp.bfloat16)
    ar, ai = halved[:, :box_edge], -halved[:, box_edge:]
    stacked = jnp.concatenate(
        [jnp.concatenate([ar, ai], 1), jnp.concatenate([ai, -ar], 1)], 0
    )
    return jnp.dot(full_map, stacked, preferred_element_type=jnp.float32).astype(jnp.bfloat16)


def fold_matrices(edge):
    half = edge // 2
    mirror = np.zeros((2 * edge, edge), np.float32)
    for l in range(1, half):
        mirror[edge - l, l] = 1.0
        mirror[2 * edge - l, half + l] = -1.0
    mirror[0, 0], mirror[edge + half, 0] = 0.5, 0.5
    mirror[edge, half], mirror[half, half] = -0.5, 0.5
    row = lax.broadcasted_iota(jnp.int32, (2 * edge, edge), 0)
    col = lax.broadcasted_iota(jnp.int32, (2 * edge, edge), 1)
    own = jnp.where(row == jnp.where(col < half, col, col + half), 1.0, 0.0)
    first = jnp.where(row == 0, 0.5, jnp.where(row == edge + half, -0.5, 0.0))
    middle = jnp.where((row == edge) | (row == half), 0.5, 0.0)
    own = jnp.where(col == 0, first, jnp.where(col == half, middle, own))
    return own.astype(jnp.bfloat16), jnp.asarray(mirror, jnp.bfloat16)


def fold_half(filtered):
    count, rows, width = filtered.shape
    edge = width // 2
    mics = lax.axis_size("mic")
    own_map, mirror_map = fold_matrices(edge)
    mirrored = jnp.einsum(
        "tkc,cl->tkl", filtered, mirror_map, preferred_element_type=jnp.float32
    ).astype(jnp.bfloat16)
    flip = np.zeros((rows, rows), np.float32)
    for i in range(1, rows):
        flip[i, rows - i] = 1.0
    turned = jnp.einsum(
        "ik,tkl->til", jnp.asarray(flip, jnp.bfloat16), mirrored, preferred_element_type=jnp.float32
    ).astype(jnp.bfloat16)
    first = lax.ppermute(mirrored[:, 0, :], "mic", [(m, (mics - m) % mics) for m in range(mics)])
    rest = lax.ppermute(turned, "mic", [(m, mics - 1 - m) for m in range(mics)])
    own = jnp.einsum("tkc,cl->tkl", filtered, own_map, preferred_element_type=jnp.float32)
    row = lax.broadcasted_iota(jnp.int32, (1, rows, 1), 1)
    other = jnp.where(row == 0, first[:, None, :].astype(jnp.float32), rest.astype(jnp.float32))
    return (own + other).astype(jnp.bfloat16)


def correlate(e, gr_ref, gi_ref, gb_ref, cs_ref, col_ref, flip_ref):
    edge = gr_ref.shape[0]
    half = edge // 2
    es = jnp.concatenate([e[:, half:], e[:, :half]], axis=1)
    gr = gr_ref[...]
    gi = gi_ref[...]
    lane = lax.broadcasted_iota(jnp.int32, (edge, edge), 1)
    low = lane < half
    narrow = lax.broadcasted_iota(jnp.int32, (edge, 128), 1)
    dr = jnp.dot(
        flip_ref[...],
        jnp.where(narrow == 0, e[:, :128], pltpu.roll(es[:, :128], 1, 1)).astype(jnp.bfloat16),
        preferred_element_type=jnp.float32,
    )
    gbr, gbi = gb_ref[:, 0:1], gb_ref[:, 1:2]
    mr, mi = dr[:, 0:1], dr[:, 1:2]
    fix_r = gbr * mr - gbi * mi
    fix_i = gbr * mi + gbi * mr
    ge, ges = gr * e, gr * es
    he, hes = gi * e, gi * es
    top = jnp.where(low, ge, -ge) + hes
    bottom = ges + jnp.where(low, -he, he)
    at_r, at_i = lane == 0, lane == half
    top = top + jnp.where(at_r, fix_r, jnp.where(at_i, fix_i, 0.0))
    bottom = bottom + jnp.where(at_r, -fix_i, jnp.where(at_i, fix_r, 0.0))
    stacked = jnp.concatenate([top.astype(jnp.bfloat16), bottom.astype(jnp.bfloat16)], axis=0)
    v = jnp.dot(cs_ref[...], stacked, preferred_element_type=jnp.float32).astype(jnp.bfloat16)
    return jnp.dot(v, col_ref[...], preferred_element_type=jnp.float32)


def accumulate(corr, peak_ref, total_ref, square_ref):
    peak_ref[...] = jnp.maximum(peak_ref[...], corr)
    total_ref[...] += corr
    square_ref[...] += corr * corr


def clear(peak_ref, total_ref, square_ref):
    peak_ref[...] = jnp.full(peak_ref.shape, -3.0e38, jnp.float32)
    total_ref[...] = jnp.zeros(total_ref.shape, jnp.float32)
    square_ref[...] = jnp.zeros(square_ref.shape, jnp.float32)


def refine_correlation(template, ctf_ref, g_ref, cs_ref):
    edge = ctf_ref.shape[0]
    gain = ctf_ref[...]
    narrow = lambda a: a.astype(jnp.bfloat16)
    fr = narrow(template[:, :edge].astype(jnp.float32) * gain).astype(jnp.float32)
    fi = narrow(template[:, edge:].astype(jnp.float32) * gain).astype(jnp.float32)
    gr = g_ref[:, :edge].astype(jnp.float32)
    gi = g_ref[:, edge:].astype(jnp.float32)
    zr = narrow(gr * fr + gi * fi)
    zi = narrow(gi * fr - gr * fi)
    ci, si = cs_ref[:, :edge], cs_ref[:, edge:]
    dot = lambda a, b: jnp.dot(a, b, preferred_element_type=jnp.float32)
    ur = narrow(dot(ci, zr) - dot(si, zi))
    ui = narrow(dot(si, zr) + dot(ci, zi))
    return dot(ur, ci) - dot(ui, si)


def search_kernel(e_ref, *refs):
    @pl.when(pl.program_id(0) == 0)
    def _():
        clear(*refs[6:])

    edge = refs[0].shape[0]
    e = e_ref[...].reshape(edge, edge).astype(jnp.float32)
    accumulate(correlate(e, *refs[:6]), *refs[6:])


def all_maps(folded, gr, gi, gb, cs, col, library, ctf, spectrum, wanted):
    count, rows, edge = folded.shape
    place = lambda axis: lax.broadcasted_iota(jnp.int32, (edge, edge), axis)
    flip = ((place(0) + place(1)) % edge == 0).astype(jnp.bfloat16)
    whole = lambda a: pl.BlockSpec(a.shape, lambda t: (0, 0))
    out = jax.ShapeDtypeStruct((edge, edge), jnp.float32)
    cost = pl.CostEstimate(
        flops=count * 350000000, bytes_accessed=count * 600000, transcendentals=0
    )
    refined = refine_map(library, ctf, spectrum, cs, wanted)
    gathered = lax.all_gather(folded, "mic", axis=1, tiled=True)[None]
    maps = pl.pallas_call(
        search_kernel,
        grid=(count,),
        in_specs=[pl.BlockSpec((1, 1, edge, edge), lambda t: (0, t, 0, 0))]
        + [whole(a) for a in (gr, gi, gb, cs, col, flip)],
        out_specs=[pl.BlockSpec((edge, edge), lambda t: (0, 0))] * 3,
        out_shape=[out] * 3,
        compiler_params=pltpu.CompilerParams(vmem_limit_bytes=40 * 1024 * 1024),
        cost_estimate=cost,
    )(gathered, gr, gi, gb, cs, col, flip)
    return merge([*maps, refined])


def refine_kernel(lib_ref, ctf_ref, g_ref, cs_ref, wanted_ref, out_ref):
    step = pl.program_id(0)
    edge = ctf_ref.shape[0]

    @pl.when(step == 0)
    def _():
        out_ref[...] = jnp.full((edge, edge), -3.0e38, jnp.float32)

    @pl.when(wanted_ref[step] > 0)
    def _():
        corr = refine_correlation(lib_ref[0], ctf_ref, g_ref, cs_ref)
        out_ref[...] = jnp.maximum(out_ref[...], corr)


def refine_map(library, ctf, spectrum, cs, wanted):
    count, edge, width = library.shape
    whole = lambda a: pl.BlockSpec(a.shape, lambda t: (0, 0))
    return pl.pallas_call(
        refine_kernel,
        grid=(count,),
        in_specs=[pl.BlockSpec((1, edge, width), lambda t: (t, 0, 0))]
        + [whole(a) for a in (ctf, spectrum, cs)]
        + [pl.BlockSpec(memory_space=pltpu.SMEM)],
        out_specs=pl.BlockSpec((edge, edge), lambda t: (0, 0)),
        out_shape=jax.ShapeDtypeStruct((edge, edge), jnp.float32),
        compiler_params=pltpu.CompilerParams(vmem_limit_bytes=40 * 1024 * 1024),
        cost_estimate=pl.CostEstimate(flops=count * 700000000, bytes_accessed=count * 1200000, transcendentals=0),
    )(library, ctf, spectrum, cs, wanted)


def join(left, right):
    right = [a.astype(jnp.float32) for a in right]
    return [
        jnp.maximum(a, b) if i in (0, 3) else a + b for i, (a, b) in enumerate(zip(left, right))
    ]


def merge(maps):
    size = lax.axis_size("orient")
    edge = maps[0].shape[0]
    half = edge // 2
    core = lax.axis_index("orient") % 2
    near = [(i, i ^ 1) for i in range(size)]
    narrow = lambda values: [a.astype(jnp.bfloat16) for a in values]
    mine = [lax.dynamic_slice_in_dim(a, core * half, half, 0) for a in maps]
    theirs = narrow(lax.dynamic_slice_in_dim(a, (1 - core) * half, half, 0) for a in maps)
    state = join(mine, lax.ppermute(jnp.stack(theirs), "orient", near))
    distance = 2
    while distance < size:
        far = [(i, i ^ distance) for i in range(size)]
        state = join(state, lax.ppermute(jnp.stack(narrow(state)), "orient", far))
        distance *= 2
    final = jnp.stack(narrow(state))
    other = lax.ppermute(final, "orient", near)
    first = jnp.where(core == 0, final, other)
    second = jnp.where(core == 0, other, final)
    return [jnp.concatenate([first[i], second[i]], 0).astype(jnp.float32) for i in range(len(maps))]


def quartered(search, library, edge):
    sizes = (lax.axis_size("mic"), lax.axis_size("orient"))
    return sizes == (8, 4) and edge == 384 and search.shape[:2] == (16, 48)


def column_plan(edge):
    half, lanes = edge // 2, 128
    plan = [("re", l) for l in range(half)]
    plan += [("im", l) for l in range(lanes, half)]
    return plan + [("im", l) for l in range(lanes)]


def quarter_tables(edge):
    half, slab, lanes = edge // 2, edge // 4, 128
    fwd_cos, fwd_sin, inv_cos, inv_sin = make_tables(edge)
    plan = column_plan(edge)
    packed = plan.index(("im", 0))
    own = np.zeros((2 * edge, edge), np.float32)
    mirror = np.zeros((2 * edge, edge), np.float32)
    freq, sign = [], []
    col = np.zeros((edge, edge), np.float32)
    for place, (kind, l) in enumerate(plan):
        freq.append(half if place == packed else l)
        sign.append(-1.0 if kind == "im" and place != packed else 1.0)
        if kind == "re":
            col[place] = inv_cos[l]
        else:
            col[place] = inv_cos[half] if place == packed else -inv_sin[l].astype(np.float32)
        if l == 0:
            continue
        if kind == "re":
            own[l, place] = 1.0
            mirror[edge - l, place] = 1.0
        else:
            own[edge + l, place] = 1.0
            mirror[2 * edge - l, place] = -1.0
    own[0, 0], own[edge + half, 0] = 0.5, -0.5
    own[edge, packed], own[half, packed] = 0.5, 0.5
    mirror[0, 0], mirror[edge + half, 0] = 0.5, 0.5
    mirror[edge, packed], mirror[half, packed] = -0.5, 0.5
    order = np.concatenate([np.arange(s * slab, (s + 1) * slab) for s in (0, 3, 1, 2)])
    flips = np.zeros((2, half + 16, half), np.float32)
    for pair, moved in enumerate((slab, 0)):
        for u in range(half):
            flips[pair, half if u == moved else u, (half - u) % half] = 1.0
    turn = np.zeros((edge, edge), np.float32)
    for i, k in enumerate(order):
        turn[i, list(order).index((edge - k) % edge)] = 1.0
    low = lambda a: jnp.asarray(np.asarray(a, np.float32), jnp.bfloat16)
    side = lambda a, b: low(np.concatenate([np.asarray(a, np.float32), np.asarray(b, np.float32)], 1))
    return dict(
        cs=side(inv_cos, inv_sin),
        cs_turned=side(inv_cos[:, order], inv_sin[:, order]),
        col=low(col),
        fold=side(own, mirror),
        flips=low(flips),
        turn=low(turn),
        full=side(fwd_cos, fwd_sin),
        full_cols=side(fwd_cos[:, freq], fwd_sin[:, freq]),
        full_rows=side(fwd_cos[order], fwd_sin[order]),
        sign=jnp.asarray(np.tile(np.asarray(sign, np.float32)[None], (8, 1))),
    )


TABLES = ("cs", "cs_turned", "col", "fold", "flips", "turn", "full", "full_cols", "full_rows", "sign")


def dot(a, b):
    return jnp.dot(a, b, preferred_element_type=jnp.float32)


def spectrum_of(image, columns, rows):
    edge = image.shape[0]
    halved = dot(image, columns).astype(jnp.bfloat16)
    ar, ai = halved[:, :edge], -halved[:, edge:]
    stacked = jnp.concatenate(
        [jnp.concatenate([ar, ai], 1), jnp.concatenate([ai, -ar], 1)], 0
    )
    return dot(rows, stacked).astype(jnp.bfloat16)


def quarter_kernel(owner_in, slot_in, image_in, search_in, library_in, ctf_in, *refs):
    inputs, refs = refs[: len(TABLES)], refs[len(TABLES) :]
    final, refined = refs[:2]
    tables, refs = refs[2 : 2 + len(TABLES)], refs[2 + len(TABLES) :]
    tab = dict(zip(TABLES, tables))
    (image, library, ctf, images, raw, folded, gains, pair_e, stack, maps, refmap,
     x_out, x_in, y_out, y_in, z_out, z_in, shared, mask_out, mask_in, cap, g_own,
     owner_ref, slot_ref) = refs[:24]
    (load_sem, raw_s, raw_r, ez_s, ez_r, ec_s, ec_r, im_s, im_r, mk_s, mk_r, sh_s, sh_r,
     x_s, x_r, y_s, y_r, z_s, z_r, ag_s, ag_r, co_s, co_r) = refs[24:]
    edge = ctf.shape[0]
    half, slab, rows = edge // 2, edge // 4, raw.shape[1] // 4
    depth = raw.shape[0]
    listed = library.shape[0]
    me, block = lax.axis_index("mic"), lax.axis_index("orient")
    z, x = me // 2, me % 2
    y, c = block // 2, block % 2
    zm, xm, ym, cm = 3 - z, 1 - x, 1 - y, 1 - c
    zn = z + 1 - 2 * (z % 2)
    upper = z // 2
    outer = (z + 1) % 4 // 2
    home = c == x
    away = c != x
    place = lambda z, x, y, c: {"mic": z * 2 + x, "orient": y * 2 + c}
    trio = [(z, xm), (zm, x), (zm, xm)]
    peers = [(y, cm), (ym, c), (ym, cm)]
    partners = [place(a, b, y, c) for a, b in trio] + [place(z, x, a, b) for a, b in peers]
    partners.append(place(zn, x, y, c))

    barrier = pltpu.get_barrier_semaphore()
    for partner in partners:
        pl.semaphore_signal(barrier, inc=1, device_id=partner, device_id_type=MESH)

    def spot(zz, xx):
        return pl.ds(pl.multiple_of(zz // 2 * slab + xx * rows, 16), rows)

    loads = [
        pltpu.make_async_copy(image_in, image, load_sem.at[0]),
        pltpu.make_async_copy(ctf_in, ctf, load_sem.at[1]),
    ]
    for i, (a, b) in enumerate(zip(inputs, tables)):
        loads.append(pltpu.make_async_copy(a, b, load_sem.at[2 + i]))
    count = len(loads)
    lib_loads = [
        pltpu.make_async_copy(library_in.at[j], library.at[j], load_sem.at[count + j])
        for j in range(listed)
    ]
    count += listed
    own_loads = [
        pltpu.make_async_copy(
            search_in.at[x * 2 * depth + upper * depth + j],
            raw.at[j, spot(z, x)],
            load_sem.at[count + j],
        )
        for j in range(depth)
    ]
    named = [
        pltpu.make_async_copy(owner_in, owner_ref, load_sem.at[count + depth]),
        pltpu.make_async_copy(slot_in, slot_ref, load_sem.at[count + depth + 1]),
    ]
    for load in named + loads + lib_loads + own_loads:
        load.start()
    for load in named:
        load.wait()

    row = lax.broadcasted_iota(jnp.int32, mask_out.shape, 0)
    mask = jnp.zeros(mask_out.shape, jnp.float32)
    for entry in range(owner_ref.shape[0]):
        key = owner_ref[entry, 0] * listed + slot_ref[entry, 0]
        mask = jnp.where(row == key, 1.0, mask)
    mask_out[...] = mask

    def remote(src, dst, send, recv, target):
        return pltpu.make_async_remote_copy(
            src_ref=src, dst_ref=dst, send_sem=send, recv_sem=recv, device_id=target, device_id_type=MESH
        )

    def send_raw(q, j):
        zz, xx = trio[q]
        return remote(
            search_in.at[xx * 2 * depth + zz // 2 * depth + j],
            raw.at[j, spot(z, x)],
            raw_s.at[q, j],
            raw_r.at[q, j],
            place(zz, xx, y, c),
        )

    def take_raw(q, j):
        zz, xx = trio[q]
        spots = raw.at[j, spot(zz, xx)]
        return remote(spots, spots, raw_s.at[q, j], raw_r.at[q, j], place(zz, xx, y, c))

    beside, across = place(z, xm, y, c), place(zm, x, y, c)
    send_own = remote(image_in, images.at[0], im_s.at[0], im_r.at[0], beside)
    send_far = remote(image_in, images.at[1], im_s.at[1], im_r.at[1], across)
    pass_far = remote(images.at[1], images.at[1], im_s.at[2], im_r.at[2], beside)

    def send_mask(q):
        yy, cc = peers[q]
        part = mask_out.at[pl.ds(pl.multiple_of((yy * 2 + cc) * listed, 8), listed)]
        return remote(part, mask_in.at[q], mk_s.at[q], mk_r.at[q], place(z, x, yy, cc))

    def send_shared(q):
        yy, cc = peers[q]
        return remote(shared.at[0], shared.at[q + 1], sh_s.at[q], sh_r.at[q], place(z, x, yy, cc))

    def send_e(j):
        part = folded.at[c, j, outer]
        return remote(part, part, ez_s.at[j], ez_r.at[j], place(zn, x, y, c))

    def take_e(j):
        part = folded.at[c, j, 1 - outer]
        return remote(part, part, ez_s.at[j], ez_r.at[j], place(zn, x, y, c))

    def core_e(j, source, pair):
        part = folded.at[source, j, pair]
        slot = pair * depth + j
        return remote(part, part, ec_s.at[slot], ec_r.at[slot], place(z, x, y, cm))

    pl.semaphore_wait(barrier, len(partners))
    for q in range(3):
        send_mask(q).start()
    for q in (1, 2, 0):
        send_raw(q, 0).start()

    @pl.when(home)
    def _():
        send_far.start()
        send_own.start()

    for q in (1, 2, 0):
        send_raw(q, 1).start()

    refmap[...] = jnp.full(refmap.shape, LOW, jnp.float32)
    for t in range(2):
        maps[t, 0] = jnp.full((edge, edge), LOW, jnp.float32)
        maps[t, 1] = jnp.zeros((edge, edge), jnp.float32)
        maps[t, 2] = jnp.zeros((edge, edge), jnp.float32)
    for load in loads:
        load.wait()
    g_own[...] = spectrum_of(image[...], tab["full"][...], tab["full"][...])
    wanted = mask_out[pl.ds(pl.multiple_of(block * listed, 8), listed), :]
    for q in range(3):
        send_mask(q).wait_recv()
        wanted = jnp.maximum(wanted, mask_in[q])
    cap[...] = jnp.where(wanted > 0.0, -LOW, LOW)
    for load in lib_loads:
        load.wait()

    def refine_some(first, last):
        def one(j, carry):
            corr = refine_correlation(library[j], ctf, g_own, tab["cs"])
            refmap[...] = jnp.maximum(refmap[...], jnp.minimum(corr, cap[pl.ds(j, 1), :]))
            return carry

        lax.fori_loop(first, last, one, 0)

    def gain_of(t, picture):
        spec = spectrum_of(picture, tab["full_cols"][...], tab["full_rows"][...]).astype(jnp.float32)
        gr, gi, sign = spec[:, :edge], spec[:, edge:], tab["sign"][0:1, :]
        gains[t, 0] = gr * sign
        gains[t, 1] = gi
        gains[t, 2] = gr
        gains[t, 3] = -gi * sign

    def fold(j):
        for q in range(3):
            take_raw(q, j).wait_recv()
        if j + 2 < depth:
            for q in (1, 2, 0):
                send_raw(q, j).wait_send()
                send_raw(q, j + 2).start()
        own_loads[j].wait()
        near = ctf[pl.ds(pl.multiple_of(outer * slab, 8), slab), :]
        far = ctf[pl.ds(pl.multiple_of((3 - outer) * slab, 8), slab), :]
        gain = jnp.concatenate([near, far], 0)
        gain = jnp.concatenate([gain, gain], 1)
        filtered = (raw[j].astype(jnp.float32) * gain).astype(jnp.bfloat16)
        both = dot(filtered, tab["fold"][...])
        turned = dot(tab["flips"][outer], both[:, edge:].astype(jnp.bfloat16))
        folded[c, j, outer, 0:half, :] = (both[:, :edge] + turned[0:half]).astype(jnp.bfloat16)
        folded[c, j, outer, half : half + 16, :] = turned[half:].astype(jnp.bfloat16)
        send_e(j).start()
        core_e(j, c, outer).start()

    def template(source, j):
        parts = [folded[source, j, p].astype(jnp.float32) for p in range(2)]
        e = jnp.concatenate(
            [
                parts[0][0:slab],
                parts[0][slab : slab + 16] + parts[1][half:],
                parts[0][slab + 16 : half],
                parts[1][0:16] + parts[0][half:],
                parts[1][16:half],
            ],
            0,
        )
        t0, t1, t2 = e[:, 0:128], e[:, 128:256], e[:, 256:384]
        back = dot(tab["turn"][...], jnp.concatenate([t0, t2], 1).astype(jnp.bfloat16))
        m0, m2 = back[:, 0:128], back[:, 128:256]
        first = lax.broadcasted_iota(jnp.int32, t0.shape, 1) == 0
        pair_e[0, :, 0:128] = jnp.where(first, 0.5 * (t0 + m0), t0)
        pair_e[0, :, 128:256] = t1
        pair_e[0, :, 256:384] = jnp.where(first, 0.5 * (t2 + m2), t2)
        pair_e[1, :, 0:128] = jnp.where(first, 0.5 * (t2 - m2), t2)
        pair_e[1, :, 128:256] = pltpu.roll(t1, 64, 1)
        pair_e[1, :, 256:384] = jnp.where(first, 0.5 * (m0 - t0), t0)
        for t in range(2):
            e, es = pair_e[0], pair_e[1]
            stack[0:edge, t * edge : (t + 1) * edge] = (gains[t, 0] * e + gains[t, 1] * es).astype(jnp.bfloat16)
            stack[edge:, t * edge : (t + 1) * edge] = (gains[t, 2] * es + gains[t, 3] * e).astype(jnp.bfloat16)
        v = dot(tab["cs_turned"][...], stack[...]).astype(jnp.bfloat16)
        for t in range(2):
            corr = dot(v[:, t * edge : (t + 1) * edge], tab["col"][...])
            maps[t, 0] = jnp.maximum(maps[t, 0], corr)
            maps[t, 1] += corr
            maps[t, 2] += corr * corr

    def templates(j):
        core_e(j, cm, outer).wait_recv()
        core_e(j, cm, 1 - outer).wait_recv()

        def one(source, carry):
            template(source, j)
            return carry

        lax.fori_loop(0, 2, one, 0)

    def arrive(j):
        take_e(j).wait_recv()
        core_e(j, c, 1 - outer).start()

    refine_some(0, listed // 4)

    @pl.when(home)
    def _():
        send_far.wait_recv()
        pass_far.start()
        images[0] = image[...]

    fold(0)
    refine_some(listed // 4, listed // 2)

    @pl.when(away)
    def _():
        send_own.wait_recv()

    gain_of(0, images[0])
    arrive(0)

    @pl.when(away)
    def _():
        pass_far.wait_recv()

    gain_of(1, images[1])
    refine_some(listed // 2, listed)
    shared[0] = refmap[...].astype(jnp.bfloat16)
    for q in range(3):
        send_shared(q).start()
    for j in range(1, depth):
        fold(j)
        templates(j - 1)
        arrive(j)
    templates(depth - 1)

    def spread(t):
        return remote(x_out.at[t], x_in.at[t], x_s.at[t], x_r.at[t], beside)

    def sides(t):
        return remote(y_out.at[t], y_in.at[t], y_s.at[t], y_r.at[t], place(z, x, ym, c))

    cross = remote(z_out, z_in, z_s, z_r, across)
    mine = pl.ds(pl.multiple_of(y * half, 16), half)
    theirs = pl.ds(pl.multiple_of(ym * half, 16), half)
    give = remote(final.at[:, mine], final.at[:, mine], ag_s, ag_r, place(z, x, ym, c))
    get = remote(final.at[:, theirs], final.at[:, theirs], ag_s, ag_r, place(z, x, ym, c))
    core = place(z, x, y, cm)
    tell = [remote(final.at[:, r], final.at[:, r], co_s.at[i], co_r.at[i], core) for i, r in enumerate((mine, theirs))]

    @pl.when(away)
    def _():
        for t in (1, 0):
            x_out[t] = maps[t].astype(jnp.bfloat16)
            spread(t).start()
        tell[0].wait_recv()
        tell[1].wait_recv()
        for t in (1, 0):
            spread(t).wait_send()

    def merge_in(t, where, piece):
        maps[t, 0, where] = jnp.maximum(maps[t, 0, where], piece[0].astype(jnp.float32))
        maps[t, 1, where] += piece[1].astype(jnp.float32)
        maps[t, 2, where] += piece[2].astype(jnp.float32)

    @pl.when(home)
    def _():
        for t in (1, 0):
            spread(t).wait_recv()
            merge_in(t, theirs, x_in[t, :, theirs])
            y_out[t] = maps[t, :, theirs].astype(jnp.bfloat16)
            sides(t).start()
            merge_in(t, mine, x_in[t, :, mine])
            if t == 1:
                continue
            sides(1).wait_recv()
            merge_in(1, mine, y_in[1])
            z_out[...] = maps[1, :, mine].astype(jnp.bfloat16)
            cross.start()
        sides(0).wait_recv()
        merge_in(0, mine, y_in[0])
        cross.wait_recv()
        merge_in(0, mine, z_in[...])
        final[:, mine] = maps[0, :, mine].astype(jnp.bfloat16)
        give.start()
        tell[0].start()
        get.wait_recv()
        tell[1].start()
        for t in range(2):
            sides(t).wait_send()
        cross.wait_send()
        give.wait_send()
        tell[0].wait_send()
        tell[1].wait_send()

    best = shared[0]
    for q in range(3):
        send_shared(q).wait_recv()
        best = jnp.maximum(best, shared[q + 1])
    refined[...] = best
    for q in range(3):
        send_shared(q).wait_send()
        send_mask(q).wait_send()
    for j in range(depth):
        for q in range(3):
            if j + 2 >= depth:
                send_raw(q, j).wait_send()
        send_e(j).wait_send()
        core_e(j, c, outer).wait_send()
        core_e(j, c, 1 - outer).wait_send()

    @pl.when(home)
    def _():
        send_own.wait_send()
        send_far.wait_send()
        pass_far.wait_send()


def quarter_maps(micrograph, search, library, ctf, ref_owner, ref_slot):
    edge = micrograph.shape[1]
    half, depth, listed = edge // 2, search.shape[0] // 4, library.shape[0]
    tables = quarter_tables(edge)
    given = [tables[name] for name in TABLES]
    any_space = pl.BlockSpec(memory_space=pl.ANY)
    vmem = pl.BlockSpec(memory_space=pltpu.VMEM)
    low, wide = jnp.bfloat16, jnp.float32
    dma = lambda *shape: pltpu.SemaphoreType.DMA(shape)
    one = pltpu.SemaphoreType.DMA
    scratch = [pltpu.VMEM(a.shape, a.dtype) for a in given]
    scratch += [
        pltpu.VMEM((edge, edge), low),
        pltpu.VMEM(library.shape, low),
        pltpu.VMEM((edge, edge), wide),
        pltpu.VMEM((2, edge, edge), low),
        pltpu.VMEM((depth, half, 2 * edge), low),
        pltpu.VMEM((2, depth, 2, half + 16, edge), low),
        pltpu.VMEM((2, 4, edge, edge), wide),
        pltpu.VMEM((2, edge, edge), wide),
        pltpu.VMEM((2 * edge, 2 * edge), low),
        pltpu.VMEM((2, 3, edge, edge), wide),
        pltpu.VMEM((edge, edge), wide),
        pltpu.VMEM((2, 3, edge, edge), low),
        pltpu.VMEM((2, 3, edge, edge), low),
        pltpu.VMEM((2, 3, half, edge), low),
        pltpu.VMEM((2, 3, half, edge), low),
        pltpu.VMEM((3, half, edge), low),
        pltpu.VMEM((3, half, edge), low),
        pltpu.VMEM((4, edge, edge), low),
        pltpu.VMEM((4 * listed, edge), wide),
        pltpu.VMEM((3, listed, edge), wide),
        pltpu.VMEM((listed, edge), wide),
        pltpu.VMEM((edge, 2 * edge), low),
        pltpu.SMEM(ref_owner.shape, jnp.int32),
        pltpu.SMEM(ref_slot.shape, jnp.int32),
        dma(2 + len(given) + listed + depth + 2),
        dma(3, depth),
        dma(3, depth),
        dma(depth),
        dma(depth),
        dma(2 * depth),
        dma(2 * depth),
        dma(3),
        dma(3),
        dma(3),
        dma(3),
        dma(3),
        dma(3),
        dma(2),
        dma(2),
        dma(2),
        dma(2),
        one,
        one,
        one,
        one,
        dma(2),
        dma(2),
    ]
    final, refined = pl.pallas_call(
        quarter_kernel,
        in_specs=[any_space] * (6 + len(given)),
        out_specs=[vmem, vmem],
        out_shape=[
            jax.ShapeDtypeStruct((3, edge, edge), low),
            jax.ShapeDtypeStruct((edge, edge), low),
        ],
        scratch_shapes=scratch,
        compiler_params=pltpu.CompilerParams(
            vmem_limit_bytes=60 * 1024 * 1024, collective_id=0, has_side_effects=True
        ),
        cost_estimate=pl.CostEstimate(flops=12000000000, bytes_accessed=12000000, transcendentals=0),
    )(ref_owner, ref_slot, micrograph, search, library, ctf, *given)
    final = final.astype(wide)
    number = float(lax.axis_size("orient") * search.shape[0])
    peak, total, square = final[0], final[1], final[2]
    return (peak, total / number, peak * lax.rsqrt(square / number + 1e-05), refined.astype(wide))


def body(micrograph, search_spectra, refine_spectra, ctf, ref_owner, ref_slot):
    edge = micrograph.shape[1]
    if quartered(search_spectra, refine_spectra, edge):
        return quarter_maps(micrograph, search_spectra, refine_spectra[0], ctf, ref_owner, ref_slot)
    half = edge // 2
    fwd_cos, fwd_sin, inv_cos, inv_sin = make_tables(edge)
    ctf_gain = jnp.concatenate([ctf, ctf], 1)
    rows_owned = search_spectra.shape[1]
    first_row = lax.axis_index("mic") * rows_owned
    own_gain = lax.dynamic_slice_in_dim(ctf_gain, first_row, rows_owned, 0)
    filtered = (search_spectra.astype(jnp.float32) * own_gain).astype(jnp.bfloat16)
    folded = fold_half(filtered)
    spectrum = forward(micrograph, fwd_cos, fwd_sin)

    library = refine_spectra[0]
    block_size = library.shape[0]
    ids = lax.all_gather(ref_owner[:, 0] * block_size + ref_slot[:, 0], "orient", axis=0, tiled=True)
    slots = lax.axis_index("orient") * block_size + jnp.arange(block_size, dtype=jnp.int32)
    wanted = jnp.any(slots[:, None] == ids[None, :], axis=1).astype(jnp.int32)
    cs = jnp.asarray(np.concatenate([inv_cos, inv_sin], 1))

    spec = spectrum.astype(jnp.float32)
    g_r, g_i = spec[:, :edge], spec[:, edge:]
    dc = jnp.stack([g_r[:, 0], g_i[:, 0]], 1)
    ny = jnp.stack([g_r[:, half], g_i[:, half]], 1)
    ga = (dc - ny) * 0.5
    gb = (dc + ny) * 0.5
    lane = lax.broadcasted_iota(jnp.int32, (edge, half), 1)
    h_r = jnp.where(lane == 0, ga[:, 0:1], g_r[:, :half])
    h_i = jnp.where(lane == 0, ga[:, 1:2], g_i[:, :half])
    gr = jnp.concatenate([h_r, h_r], 1)
    gi = jnp.concatenate([h_i, h_i], 1)
    sin_rows = -inv_sin[:half]
    sin_rows[0] = inv_cos[half]
    col = jnp.asarray(np.concatenate([inv_cos[:half], sin_rows], 0))
    peak, total, square, refined = all_maps(
        folded, gr, gi, gb, cs, col, library, ctf, spectrum, wanted
    )
    count = float(lax.axis_size("orient") * search_spectra.shape[0])
    return (peak, total / count, peak * lax.rsqrt(square / count + 1e-05), refined)


def solution(mesh):
    in_specs = (
        P("mic", None),
        P("orient", "mic", None),
        P("mic", "orient", None, None),
        P(),
        P(("mic", "orient"), None),
        P(("mic", "orient"), None),
    )
    out_specs = (P("mic", None), P("mic", None), P("mic", None), P("mic", None))
    return jax.shard_map(body, mesh=mesh, in_specs=in_specs, out_specs=out_specs, check_vma=False)
```

```python
import functools
import math

import jax
import jax.numpy as jnp
import numpy as np
from jax import lax
from jax.experimental import pallas as pl
from jax.experimental.pallas import tpu as pltpu
from jax.sharding import PartitionSpec as P

MESH = pl.DeviceIdType.MESH
LOW = -3.0e38


def make_tables(box_edge):
    positions = np.arange(box_edge, dtype=np.int32)
    products = positions[:, None] * positions[None, :] % box_edge
    angles = products.astype(np.float32) * np.float32(2.0 * math.pi / box_edge)
    cosine = np.cos(angles)
    sines = np.sin(angles)
    narrow = lambda a: a.astype(np.float32).astype(jnp.bfloat16)
    fwd_cos, fwd_sin = narrow(cosine), narrow(sines)
    inv_cos = narrow(cosine / np.float32(box_edge))
    inv_sin = narrow(sines / np.float32(box_edge))
    return (fwd_cos, fwd_sin, inv_cos, inv_sin)


def forward(tile_image, fwd_cos, fwd_sin):
    box_edge = tile_image.shape[0]
    full_map = jnp.asarray(np.concatenate([fwd_cos, fwd_sin], 1))
    halved = jnp.dot(tile_image, full_map, preferred_element_type=jnp.float32).astype(jnp.bfloat16)
    ar, ai = halved[:, :box_edge], -halved[:, box_edge:]
    stacked = jnp.concatenate(
        [jnp.concatenate([ar, ai], 1), jnp.concatenate([ai, -ar], 1)], 0
    )
    return jnp.dot(full_map, stacked, preferred_element_type=jnp.float32).astype(jnp.bfloat16)


def fold_matrices(edge):
    half = edge // 2
    mirror = np.zeros((2 * edge, edge), np.float32)
    for l in range(1, half):
        mirror[edge - l, l] = 1.0
        mirror[2 * edge - l, half + l] = -1.0
    mirror[0, 0], mirror[edge + half, 0] = 0.5, 0.5
    mirror[edge, half], mirror[half, half] = -0.5, 0.5
    row = lax.broadcasted_iota(jnp.int32, (2 * edge, edge), 0)
    col = lax.broadcasted_iota(jnp.int32, (2 * edge, edge), 1)
    own = jnp.where(row == jnp.where(col < half, col, col + half), 1.0, 0.0)
    first = jnp.where(row == 0, 0.5, jnp.where(row == edge + half, -0.5, 0.0))
    middle = jnp.where((row == edge) | (row == half), 0.5, 0.0)
    own = jnp.where(col == 0, first, jnp.where(col == half, middle, own))
    return own.astype(jnp.bfloat16), jnp.asarray(mirror, jnp.bfloat16)


def fold_half(filtered):
    count, rows, width = filtered.shape
    edge = width // 2
    mics = lax.axis_size("mic")
    own_map, mirror_map = fold_matrices(edge)
    mirrored = jnp.einsum(
        "tkc,cl->tkl", filtered, mirror_map, preferred_element_type=jnp.float32
    ).astype(jnp.bfloat16)
    flip = np.zeros((rows, rows), np.float32)
    for i in range(1, rows):
        flip[i, rows - i] = 1.0
    turned = jnp.einsum(
        "ik,tkl->til", jnp.asarray(flip, jnp.bfloat16), mirrored, preferred_element_type=jnp.float32
    ).astype(jnp.bfloat16)
    first = lax.ppermute(mirrored[:, 0, :], "mic", [(m, (mics - m) % mics) for m in range(mics)])
    rest = lax.ppermute(turned, "mic", [(m, mics - 1 - m) for m in range(mics)])
    own = jnp.einsum("tkc,cl->tkl", filtered, own_map, preferred_element_type=jnp.float32)
    row = lax.broadcasted_iota(jnp.int32, (1, rows, 1), 1)
    other = jnp.where(row == 0, first[:, None, :].astype(jnp.float32), rest.astype(jnp.float32))
    return (own + other).astype(jnp.bfloat16)


def correlate(e, gr_ref, gi_ref, gb_ref, cs_ref, col_ref, flip_ref):
    edge = gr_ref.shape[0]
    half = edge // 2
    es = jnp.concatenate([e[:, half:], e[:, :half]], axis=1)
    gr = gr_ref[...]
    gi = gi_ref[...]
    lane = lax.broadcasted_iota(jnp.int32, (edge, edge), 1)
    low = lane < half
    narrow = lax.broadcasted_iota(jnp.int32, (edge, 128), 1)
    dr = jnp.dot(
        flip_ref[...],
        jnp.where(narrow == 0, e[:, :128], pltpu.roll(es[:, :128], 1, 1)).astype(jnp.bfloat16),
        preferred_element_type=jnp.float32,
    )
    gbr, gbi = gb_ref[:, 0:1], gb_ref[:, 1:2]
    mr, mi = dr[:, 0:1], dr[:, 1:2]
    fix_r = gbr * mr - gbi * mi
    fix_i = gbr * mi + gbi * mr
    ge, ges = gr * e, gr * es
    he, hes = gi * e, gi * es
    top = jnp.where(low, ge, -ge) + hes
    bottom = ges + jnp.where(low, -he, he)
    at_r, at_i = lane == 0, lane == half
    top = top + jnp.where(at_r, fix_r, jnp.where(at_i, fix_i, 0.0))
    bottom = bottom + jnp.where(at_r, -fix_i, jnp.where(at_i, fix_r, 0.0))
    stacked = jnp.concatenate([top.astype(jnp.bfloat16), bottom.astype(jnp.bfloat16)], axis=0)
    v = jnp.dot(cs_ref[...], stacked, preferred_element_type=jnp.float32).astype(jnp.bfloat16)
    return jnp.dot(v, col_ref[...], preferred_element_type=jnp.float32)


def accumulate(corr, peak_ref, total_ref, square_ref):
    peak_ref[...] = jnp.maximum(peak_ref[...], corr)
    total_ref[...] += corr
    square_ref[...] += corr * corr


def clear(peak_ref, total_ref, square_ref):
    peak_ref[...] = jnp.full(peak_ref.shape, -3.0e38, jnp.float32)
    total_ref[...] = jnp.zeros(total_ref.shape, jnp.float32)
    square_ref[...] = jnp.zeros(square_ref.shape, jnp.float32)


def refine_correlation(template, ctf_ref, g_ref, cs_ref):
    edge = ctf_ref.shape[0]
    gain = ctf_ref[...]
    narrow = lambda a: a.astype(jnp.bfloat16)
    fr = narrow(template[:, :edge].astype(jnp.float32) * gain).astype(jnp.float32)
    fi = narrow(template[:, edge:].astype(jnp.float32) * gain).astype(jnp.float32)
    gr = g_ref[:, :edge].astype(jnp.float32)
    gi = g_ref[:, edge:].astype(jnp.float32)
    zr = narrow(gr * fr + gi * fi)
    zi = narrow(gi * fr - gr * fi)
    ci, si = cs_ref[:, :edge], cs_ref[:, edge:]
    dot = lambda a, b: jnp.dot(a, b, preferred_element_type=jnp.float32)
    ur = narrow(dot(ci, zr) - dot(si, zi))
    ui = narrow(dot(si, zr) + dot(ci, zi))
    return dot(ur, ci) - dot(ui, si)


def search_kernel(e_ref, *refs):
    @pl.when(pl.program_id(0) == 0)
    def _():
        clear(*refs[6:])

    edge = refs[0].shape[0]
    e = e_ref[...].reshape(edge, edge).astype(jnp.float32)
    accumulate(correlate(e, *refs[:6]), *refs[6:])


def all_maps(folded, gr, gi, gb, cs, col, library, ctf, spectrum, wanted):
    count, rows, edge = folded.shape
    place = lambda axis: lax.broadcasted_iota(jnp.int32, (edge, edge), axis)
    flip = ((place(0) + place(1)) % edge == 0).astype(jnp.bfloat16)
    whole = lambda a: pl.BlockSpec(a.shape, lambda t: (0, 0))
    out = jax.ShapeDtypeStruct((edge, edge), jnp.float32)
    cost = pl.CostEstimate(
        flops=count * 350000000, bytes_accessed=count * 600000, transcendentals=0
    )
    refined = refine_map(library, ctf, spectrum, cs, wanted)
    gathered = lax.all_gather(folded, "mic", axis=1, tiled=True)[None]
    maps = pl.pallas_call(
        search_kernel,
        grid=(count,),
        in_specs=[pl.BlockSpec((1, 1, edge, edge), lambda t: (0, t, 0, 0))]
        + [whole(a) for a in (gr, gi, gb, cs, col, flip)],
        out_specs=[pl.BlockSpec((edge, edge), lambda t: (0, 0))] * 3,
        out_shape=[out] * 3,
        compiler_params=pltpu.CompilerParams(vmem_limit_bytes=40 * 1024 * 1024),
        cost_estimate=cost,
    )(gathered, gr, gi, gb, cs, col, flip)
    return merge([*maps, refined])


def refine_kernel(lib_ref, ctf_ref, g_ref, cs_ref, wanted_ref, out_ref):
    step = pl.program_id(0)
    edge = ctf_ref.shape[0]

    @pl.when(step == 0)
    def _():
        out_ref[...] = jnp.full((edge, edge), -3.0e38, jnp.float32)

    @pl.when(wanted_ref[step] > 0)
    def _():
        corr = refine_correlation(lib_ref[0], ctf_ref, g_ref, cs_ref)
        out_ref[...] = jnp.maximum(out_ref[...], corr)


def refine_map(library, ctf, spectrum, cs, wanted):
    count, edge, width = library.shape
    whole = lambda a: pl.BlockSpec(a.shape, lambda t: (0, 0))
    return pl.pallas_call(
        refine_kernel,
        grid=(count,),
        in_specs=[pl.BlockSpec((1, edge, width), lambda t: (t, 0, 0))]
        + [whole(a) for a in (ctf, spectrum, cs)]
        + [pl.BlockSpec(memory_space=pltpu.SMEM)],
        out_specs=pl.BlockSpec((edge, edge), lambda t: (0, 0)),
        out_shape=jax.ShapeDtypeStruct((edge, edge), jnp.float32),
        compiler_params=pltpu.CompilerParams(vmem_limit_bytes=40 * 1024 * 1024),
        cost_estimate=pl.CostEstimate(flops=count * 700000000, bytes_accessed=count * 1200000, transcendentals=0),
    )(library, ctf, spectrum, cs, wanted)


def join(left, right):
    right = [a.astype(jnp.float32) for a in right]
    return [
        jnp.maximum(a, b) if i in (0, 3) else a + b for i, (a, b) in enumerate(zip(left, right))
    ]


def merge(maps):
    size = lax.axis_size("orient")
    edge = maps[0].shape[0]
    half = edge // 2
    core = lax.axis_index("orient") % 2
    near = [(i, i ^ 1) for i in range(size)]
    narrow = lambda values: [a.astype(jnp.bfloat16) for a in values]
    mine = [lax.dynamic_slice_in_dim(a, core * half, half, 0) for a in maps]
    theirs = narrow(lax.dynamic_slice_in_dim(a, (1 - core) * half, half, 0) for a in maps)
    state = join(mine, lax.ppermute(jnp.stack(theirs), "orient", near))
    distance = 2
    while distance < size:
        far = [(i, i ^ distance) for i in range(size)]
        state = join(state, lax.ppermute(jnp.stack(narrow(state)), "orient", far))
        distance *= 2
    final = jnp.stack(narrow(state))
    other = lax.ppermute(final, "orient", near)
    first = jnp.where(core == 0, final, other)
    second = jnp.where(core == 0, other, final)
    return [jnp.concatenate([first[i], second[i]], 0).astype(jnp.float32) for i in range(len(maps))]


def quartered(search, library, edge):
    sizes = (lax.axis_size("mic"), lax.axis_size("orient"))
    return sizes == (8, 4) and edge == 384 and search.shape[:2] == (16, 48)


def column_plan(edge):
    half, lanes = edge // 2, 128
    plan = [("re", l) for l in range(half)]
    plan += [("im", l) for l in range(lanes, half)]
    return plan + [("im", l) for l in range(lanes)]


def quarter_tables(edge):
    half, slab, lanes = edge // 2, edge // 4, 128
    fwd_cos, fwd_sin, inv_cos, inv_sin = make_tables(edge)
    plan = column_plan(edge)
    packed = plan.index(("im", 0))
    own = np.zeros((2 * edge, edge), np.float32)
    mirror = np.zeros((2 * edge, edge), np.float32)
    freq, sign = [], []
    col = np.zeros((edge, edge), np.float32)
    for place, (kind, l) in enumerate(plan):
        freq.append(half if place == packed else l)
        sign.append(-1.0 if kind == "im" and place != packed else 1.0)
        if kind == "re":
            col[place] = inv_cos[l]
        else:
            col[place] = inv_cos[half] if place == packed else -inv_sin[l].astype(np.float32)
        if l == 0:
            continue
        if kind == "re":
            own[l, place] = 1.0
            mirror[edge - l, place] = 1.0
        else:
            own[edge + l, place] = 1.0
            mirror[2 * edge - l, place] = -1.0
    own[0, 0], own[edge + half, 0] = 0.5, -0.5
    own[edge, packed], own[half, packed] = 0.5, 0.5
    mirror[0, 0], mirror[edge + half, 0] = 0.5, 0.5
    mirror[edge, packed], mirror[half, packed] = -0.5, 0.5
    order = np.concatenate([np.arange(s * slab, (s + 1) * slab) for s in (0, 3, 1, 2)])
    flips = np.zeros((2, half + 16, half), np.float32)
    for pair, moved in enumerate((slab, 0)):
        for u in range(half):
            flips[pair, half if u == moved else u, (half - u) % half] = 1.0
    turn = np.zeros((edge, edge), np.float32)
    for i, k in enumerate(order):
        turn[i, list(order).index((edge - k) % edge)] = 1.0
    low = lambda a: jnp.asarray(np.asarray(a, np.float32), jnp.bfloat16)
    side = lambda a, b: low(np.concatenate([np.asarray(a, np.float32), np.asarray(b, np.float32)], 1))
    return dict(
        cs=side(inv_cos, inv_sin),
        cs_turned=side(inv_cos[:, order], inv_sin[:, order]),
        col=low(col),
        fold=side(own, mirror),
        flips=low(flips),
        turn=low(turn),
        full=side(fwd_cos, fwd_sin),
        full_cols=side(fwd_cos[:, freq], fwd_sin[:, freq]),
        full_rows=side(fwd_cos[order], fwd_sin[order]),
        sign=jnp.asarray(np.tile(np.asarray(sign, np.float32)[None], (8, 1))),
    )


TABLES = ("cs", "cs_turned", "col", "fold", "flips", "turn", "full", "full_cols", "full_rows", "sign")


def dot(a, b):
    return jnp.dot(a, b, preferred_element_type=jnp.float32)


def spectrum_of(image, columns, rows):
    edge = image.shape[0]
    halved = dot(image, columns).astype(jnp.bfloat16)
    ar, ai = halved[:, :edge], -halved[:, edge:]
    stacked = jnp.concatenate(
        [jnp.concatenate([ar, ai], 1), jnp.concatenate([ai, -ar], 1)], 0
    )
    return dot(rows, stacked).astype(jnp.bfloat16)


def quarter_kernel(ids_in, image_in, search_in, library_in, ctf_in, *refs):
    inputs, refs = refs[: len(TABLES)], refs[len(TABLES) :]
    final, refined = refs[:2]
    tables, refs = refs[2 : 2 + len(TABLES)], refs[2 + len(TABLES) :]
    tab = dict(zip(TABLES, tables))
    (image, library, ctf, images, raw, folded, gains, pair_e, stack, maps, refmap,
     x_out, x_in, y_out, y_in, z_out, z_in, shared, mask_out, mask_in, cap, g_own,
     ids_ref) = refs[:23]
    (load_sem, raw_s, raw_r, ez_s, ez_r, ec_s, ec_r, im_s, im_r, mk_s, mk_r, sh_s, sh_r,
     x_s, x_r, y_s, y_r, z_s, z_r, ag_s, ag_r, co_s, co_r) = refs[23:]
    edge = ctf.shape[0]
    half, slab, rows = edge // 2, edge // 4, raw.shape[1] // 4
    depth = raw.shape[0]
    listed = library.shape[0]
    me, block = lax.axis_index("mic"), lax.axis_index("orient")
    z, x = me // 2, me % 2
    y, c = block // 2, block % 2
    zm, xm, ym, cm = 3 - z, 1 - x, 1 - y, 1 - c
    zn = z + 1 - 2 * (z % 2)
    upper = z // 2
    outer = (z + 1) % 4 // 2
    home = c == x
    away = c != x
    place = lambda z, x, y, c: {"mic": z * 2 + x, "orient": y * 2 + c}
    trio = [(z, xm), (zm, x), (zm, xm)]
    peers = [(y, cm), (ym, c), (ym, cm)]
    partners = [place(a, b, y, c) for a, b in trio] + [place(z, x, a, b) for a, b in peers]
    partners.append(place(zn, x, y, c))

    barrier = pltpu.get_barrier_semaphore()
    for partner in partners:
        pl.semaphore_signal(barrier, inc=1, device_id=partner, device_id_type=MESH)

    def spot(zz, xx):
        return pl.ds(pl.multiple_of(zz // 2 * slab + xx * rows, 16), rows)

    loads = [
        pltpu.make_async_copy(image_in, image, load_sem.at[0]),
        pltpu.make_async_copy(ctf_in, ctf, load_sem.at[1]),
    ]
    for i, (a, b) in enumerate(zip(inputs, tables)):
        loads.append(pltpu.make_async_copy(a, b, load_sem.at[2 + i]))
    count = len(loads)
    lib_loads = [
        pltpu.make_async_copy(library_in.at[j], library.at[j], load_sem.at[count + j])
        for j in range(listed)
    ]
    count += listed
    own_loads = [
        pltpu.make_async_copy(
            search_in.at[x * 2 * depth + upper * depth + j],
            raw.at[j, spot(z, x)],
            load_sem.at[count + j],
        )
        for j in range(depth)
    ]
    named = [pltpu.make_async_copy(ids_in, ids_ref, load_sem.at[count + depth])]
    for load in named + loads + lib_loads + own_loads:
        load.start()
    for load in named:
        load.wait()

    row = lax.broadcasted_iota(jnp.int32, mask_out.shape, 0)
    mask = jnp.zeros(mask_out.shape, jnp.float32)
    for entry in range(ids_ref.shape[1]):
        mask = jnp.where(row == ids_ref[0, entry], 1.0, mask)
    mask_out[...] = mask

    def remote(src, dst, send, recv, target):
        return pltpu.make_async_remote_copy(
            src_ref=src, dst_ref=dst, send_sem=send, recv_sem=recv, device_id=target, device_id_type=MESH
        )

    def send_raw(q, j):
        zz, xx = trio[q]
        return remote(
            search_in.at[xx * 2 * depth + zz // 2 * depth + j],
            raw.at[j, spot(z, x)],
            raw_s.at[q, j],
            raw_r.at[q, j],
            place(zz, xx, y, c),
        )

    def take_raw(q, j):
        zz, xx = trio[q]
        spots = raw.at[j, spot(zz, xx)]
        return remote(spots, spots, raw_s.at[q, j], raw_r.at[q, j], place(zz, xx, y, c))

    beside, across = place(z, xm, y, c), place(zm, x, y, c)
    send_own = remote(image_in, images.at[0], im_s.at[0], im_r.at[0], beside)
    mine = pl.ds(pl.multiple_of(y * half, 16), half)
    theirs = pl.ds(pl.multiple_of(ym * half, 16), half)
    twin = place(z, x, ym, c)
    core = place(z, x, y, cm)
    send_far = remote(image_in.at[mine], images.at[1, mine], im_s.at[1], im_r.at[1], across)
    pass_far = remote(images.at[1, mine], images.at[1, mine], im_s.at[2], im_r.at[2], beside)
    pass_twin = remote(images.at[1, mine], images.at[1, mine], im_s.at[3], im_r.at[3], twin)
    take_twin = remote(images.at[1, theirs], images.at[1, theirs], im_s.at[3], im_r.at[3], twin)

    def send_mask(q):
        yy, cc = peers[q]
        part = mask_out.at[pl.ds(pl.multiple_of((yy * 2 + cc) * listed, 8), listed)]
        return remote(part, mask_in.at[q], mk_s.at[q], mk_r.at[q], place(z, x, yy, cc))

    part_c = pl.ds(pl.multiple_of(c * half, 16), half)
    part_o = pl.ds(pl.multiple_of(cm * half, 16), half)
    share_core = remote(shared.at[0], shared.at[1], sh_s.at[0], sh_r.at[0], core)
    share_twin = remote(shared.at[2, part_c], shared.at[3, part_c], sh_s.at[1], sh_r.at[1], twin)
    share_last = remote(refined.at[part_c], refined.at[part_c], sh_s.at[2], sh_r.at[2], core)
    take_last = remote(refined.at[part_o], refined.at[part_o], sh_s.at[2], sh_r.at[2], core)

    def send_e(j):
        part = folded.at[c, j, outer]
        return remote(part, part, ez_s.at[j], ez_r.at[j], place(zn, x, y, c))

    def take_e(j):
        part = folded.at[c, j, 1 - outer]
        return remote(part, part, ez_s.at[j], ez_r.at[j], place(zn, x, y, c))

    def core_e(j, source, pair):
        part = folded.at[source, j, pair]
        slot = pair * depth + j
        return remote(part, part, ec_s.at[slot], ec_r.at[slot], place(z, x, y, cm))

    pl.semaphore_wait(barrier, len(partners))
    for q in range(3):
        send_mask(q).start()
    pl.when(home)(lambda: send_far.start())
    for q in (1, 2, 0):
        send_raw(q, 0).start()
    pl.when(home)(lambda: send_own.start())
    for q in (1, 2, 0):
        send_raw(q, 1).start()

    refmap[...] = jnp.full(refmap.shape, LOW, jnp.float32)
    for t in range(2):
        maps[t, 0] = jnp.full((edge, edge), LOW, jnp.float32)
        maps[t, 1] = jnp.zeros((edge, edge), jnp.float32)
        maps[t, 2] = jnp.zeros((edge, edge), jnp.float32)
    for load in loads:
        load.wait()
    g_own[...] = spectrum_of(image[...], tab["full"][...], tab["full"][...])
    wanted = mask_out[pl.ds(pl.multiple_of(block * listed, 8), listed), :]
    for q in range(3):
        send_mask(q).wait_recv()
        wanted = jnp.maximum(wanted, mask_in[q])
    cap[...] = jnp.where(wanted > 0.0, -LOW, LOW)
    for load in lib_loads:
        load.wait()

    def refine_some(first, last):
        def one(j, carry):
            corr = refine_correlation(library[j], ctf, g_own, tab["cs"])
            refmap[...] = jnp.maximum(refmap[...], jnp.minimum(corr, cap[pl.ds(j, 1), :]))
            return carry

        lax.fori_loop(first, last, one, 0)

    def gain_of(t, picture):
        spec = spectrum_of(picture, tab["full_cols"][...], tab["full_rows"][...]).astype(jnp.float32)
        gr, gi, sign = spec[:, :edge], spec[:, edge:], tab["sign"][0:1, :]
        gains[t, 0] = gr * sign
        gains[t, 1] = gi
        gains[t, 2] = gr
        gains[t, 3] = -gi * sign

    def fold(j):
        for q in range(3):
            take_raw(q, j).wait_recv()
        if j + 2 < depth:
            for q in (1, 2, 0):
                send_raw(q, j).wait_send()
                send_raw(q, j + 2).start()
        own_loads[j].wait()
        near = ctf[pl.ds(pl.multiple_of(outer * slab, 8), slab), :]
        far = ctf[pl.ds(pl.multiple_of((3 - outer) * slab, 8), slab), :]
        gain = jnp.concatenate([near, far], 0)
        gain = jnp.concatenate([gain, gain], 1)
        filtered = (raw[j].astype(jnp.float32) * gain).astype(jnp.bfloat16)
        both = dot(filtered, tab["fold"][...])
        turned = dot(tab["flips"][outer], both[:, edge:].astype(jnp.bfloat16))
        folded[c, j, outer, 0:half, :] = (both[:, :edge] + turned[0:half]).astype(jnp.bfloat16)
        folded[c, j, outer, half : half + 16, :] = turned[half:].astype(jnp.bfloat16)
        send_e(j).start()
        core_e(j, c, outer).start()

    def prepare_one(source, j):
        parts = [folded[source, j, p].astype(jnp.float32) for p in range(2)]
        e = jnp.concatenate(
            [
                parts[0][0:slab],
                parts[0][slab : slab + 16] + parts[1][half:],
                parts[0][slab + 16 : half],
                parts[1][0:16] + parts[0][half:],
                parts[1][16:half],
            ],
            0,
        )
        t0, t1, t2 = e[:, 0:128], e[:, 128:256], e[:, 256:384]
        back = dot(tab["turn"][...], jnp.concatenate([t0, t2], 1).astype(jnp.bfloat16))
        m0, m2 = back[:, 0:128], back[:, 128:256]
        first = lax.broadcasted_iota(jnp.int32, t0.shape, 1) == 0
        pair_e[source, 0, :, 0:128] = jnp.where(first, 0.5 * (t0 + m0), t0)
        pair_e[source, 0, :, 128:256] = t1
        pair_e[source, 0, :, 256:384] = jnp.where(first, 0.5 * (t2 + m2), t2)
        pair_e[source, 1, :, 0:128] = jnp.where(first, 0.5 * (t2 - m2), t2)
        pair_e[source, 1, :, 128:256] = pltpu.roll(t1, 64, 1)
        pair_e[source, 1, :, 256:384] = jnp.where(first, 0.5 * (m0 - t0), t0)

    def prepare(j):
        prepare_one(0, j)
        prepare_one(1, j)

    def search(t):
        for n in range(2):
            e, es = pair_e[n, 0], pair_e[n, 1]
            stack[0:edge, n * edge : (n + 1) * edge] = (gains[t, 0] * e + gains[t, 1] * es).astype(jnp.bfloat16)
            stack[edge:, n * edge : (n + 1) * edge] = (gains[t, 2] * es + gains[t, 3] * e).astype(jnp.bfloat16)
        v = dot(tab["cs_turned"][...], stack[...]).astype(jnp.bfloat16)
        one = dot(v[:, 0:edge], tab["col"][...])
        two = dot(v[:, edge:], tab["col"][...])
        maps[t, 0] = jnp.maximum(maps[t, 0], jnp.maximum(one, two))
        maps[t, 1] += one + two
        maps[t, 2] += one * one + two * two

    def await_core(j):
        core_e(j, cm, outer).wait_recv()
        core_e(j, cm, 1 - outer).wait_recv()

    def templates(j):
        await_core(j)
        prepare(j)

        def one(t, carry):
            search(t)
            return carry

        lax.fori_loop(0, 2, one, 0)

    def arrive(j):
        take_e(j).wait_recv()
        core_e(j, c, 1 - outer).start()

    eighth = lambda n: listed * n // 8
    refine_some(0, eighth(2))

    @pl.when(home)
    def _():
        send_far.wait_recv()
        pass_far.start()
        pass_twin.start()
        images[0] = image[...]

    refine_some(eighth(2), eighth(4))
    fold(0)

    @pl.when(away)
    def _():
        pass_far.wait_recv()
        pass_twin.start()
        send_own.wait_recv()

    gain_of(0, images[0])
    refine_some(eighth(4), eighth(5))
    fold(1)
    arrive(0)
    take_twin.wait_recv()
    gain_of(1, images[1])
    templates(0)
    arrive(1)
    fold(2)
    templates(1)
    refine_some(eighth(5), listed)
    shared[0] = refmap[...].astype(jnp.bfloat16)
    share_core.start()
    fold(3)
    arrive(2)
    share_core.wait_recv()
    shared[2] = jnp.maximum(shared[0], shared[1])
    share_twin.start()
    templates(2)
    arrive(3)
    share_twin.wait_recv()
    refined[part_c] = jnp.maximum(shared[2, part_c], shared[3, part_c])
    share_last.start()
    await_core(3)
    prepare(3)

    quarter = half // 2
    keep = [pl.ds(pl.multiple_of(a * half + y * quarter, 16), quarter) for a in range(2)]
    give = [pl.ds(pl.multiple_of(a * half + ym * quarter, 16), quarter) for a in range(2)]
    upper_rows = slice(0, half)

    def x_send(t, part):
        rows = pl.ds(0, half) if part == 0 else keep[1]
        return remote(x_out.at[t, :, rows], x_in.at[t, :, rows], x_s.at[t, part], x_r.at[t, part], beside)

    def y_send(t, part):
        return remote(y_out.at[t, part], y_in.at[t, part], y_s.at[t, part], y_r.at[t, part], twin)

    def z_send(part):
        return remote(z_out.at[part], z_in.at[part], z_s.at[part], z_r.at[part], across)

    def final_send(part):
        return remote(final.at[:, keep[part]], final.at[:, keep[part]], ag_s.at[part], ag_r.at[part], twin)

    def final_take(part):
        return remote(final.at[:, give[part]], final.at[:, give[part]], ag_s.at[part], ag_r.at[part], twin)

    def core_final(part, where):
        rows = (keep, give)[where][part]
        slot = where * 2 + part
        return remote(final.at[:, rows], final.at[:, rows], co_s.at[slot], co_r.at[slot], core)

    def merge_in(t, where, piece):
        maps[t, 0, where] = jnp.maximum(maps[t, 0, where], piece[0].astype(jnp.float32))
        maps[t, 1, where] += piece[1].astype(jnp.float32)
        maps[t, 2, where] += piece[2].astype(jnp.float32)

    for t in (1, 0):
        search(t)
        y_out[t, 1] = maps[t, :, give[1]].astype(jnp.bfloat16)
        y_send(t, 1).start()

        @pl.when(away)
        def _(t=t):
            x_out[t, :, upper_rows] = maps[t, :, upper_rows].astype(jnp.bfloat16)
            x_send(t, 0).start()

        @pl.when(home)
        def _(t=t):
            x_send(t, 0).wait_recv()
            merge_in(t, give[0], x_in[t, :, give[0]])
            y_out[t, 0] = maps[t, :, give[0]].astype(jnp.bfloat16)
            y_send(t, 0).start()
            merge_in(t, keep[0], x_in[t, :, keep[0]])

        y_send(t, 1).wait_recv()
        merge_in(t, keep[1], y_in[t, 1])

        @pl.when(away)
        def _(t=t):
            x_out[t, :, keep[1]] = maps[t, :, keep[1]].astype(jnp.bfloat16)
            x_send(t, 1).start()

        @pl.when(home)
        def _(t=t):
            y_send(t, 0).wait_recv()
            merge_in(t, keep[0], y_in[t, 0])
            if t == 1:
                z_out[0] = maps[1, :, keep[0]].astype(jnp.bfloat16)
                z_send(0).start()
            x_send(t, 1).wait_recv()
            merge_in(t, keep[1], x_in[t, :, keep[1]])
            if t == 1:
                z_out[1] = maps[1, :, keep[1]].astype(jnp.bfloat16)
                z_send(1).start()

    @pl.when(home)
    def _():
        for part in range(2):
            z_send(part).wait_recv()
            merge_in(0, keep[part], z_in[part])
            final[:, keep[part]] = maps[0, :, keep[part]].astype(jnp.bfloat16)
            final_send(part).start()
            core_final(part, 0).start()
        for part in range(2):
            final_take(part).wait_recv()
            core_final(part, 1).start()
        for part in range(2):
            y_send(0, part).wait_send()
            y_send(1, part).wait_send()
            z_send(part).wait_send()
            final_send(part).wait_send()
            core_final(part, 0).wait_send()
            core_final(part, 1).wait_send()

    @pl.when(away)
    def _():
        for part in range(2):
            x_send(0, part).wait_send()
            x_send(1, part).wait_send()
            y_send(part, 1).wait_send()
        for part in range(2):
            core_final(part, 0).wait_recv()
        for part in range(2):
            core_final(part, 1).wait_recv()

    take_last.wait_recv()
    share_core.wait_send()
    share_twin.wait_send()
    share_last.wait_send()
    pass_twin.wait_send()
    for q in range(3):
        send_mask(q).wait_send()
    for j in range(depth):
        for q in range(3):
            if j + 2 >= depth:
                send_raw(q, j).wait_send()
        send_e(j).wait_send()
        core_e(j, c, outer).wait_send()
        core_e(j, c, 1 - outer).wait_send()

    @pl.when(home)
    def _():
        send_own.wait_send()
        send_far.wait_send()
        pass_far.wait_send()


def finish_kernel(number, final, best, peak, mean, scaled, refined):
    top = final[0].astype(jnp.float32)
    peak[...] = top
    mean[...] = final[1].astype(jnp.float32) / number
    scaled[...] = top * lax.rsqrt(final[2].astype(jnp.float32) / number + 1e-05)
    refined[...] = best[...].astype(jnp.float32)


def quarter_maps(micrograph, search, library, ctf, ref_owner, ref_slot):
    edge = micrograph.shape[1]
    half, depth, listed = edge // 2, search.shape[0] // 4, library.shape[0]
    ids = (ref_owner * listed + ref_slot).reshape(1, -1)
    tables = quarter_tables(edge)
    given = [tables[name] for name in TABLES]
    any_space = pl.BlockSpec(memory_space=pl.ANY)
    vmem = pl.BlockSpec(memory_space=pltpu.VMEM)
    low, wide = jnp.bfloat16, jnp.float32
    dma = lambda *shape: pltpu.SemaphoreType.DMA(shape)
    scratch = [pltpu.VMEM(a.shape, a.dtype) for a in given]
    scratch += [
        pltpu.VMEM((edge, edge), low),
        pltpu.VMEM(library.shape, low),
        pltpu.VMEM((edge, edge), wide),
        pltpu.VMEM((2, edge, edge), low),
        pltpu.VMEM((depth, half, 2 * edge), low),
        pltpu.VMEM((2, depth, 2, half + 16, edge), low),
        pltpu.VMEM((2, 4, edge, edge), wide),
        pltpu.VMEM((2, 2, edge, edge), wide),
        pltpu.VMEM((2 * edge, 2 * edge), low),
        pltpu.VMEM((2, 3, edge, edge), wide),
        pltpu.VMEM((edge, edge), wide),
        pltpu.VMEM((2, 3, edge, edge), low),
        pltpu.VMEM((2, 3, edge, edge), low),
        pltpu.VMEM((2, 2, 3, half // 2, edge), low),
        pltpu.VMEM((2, 2, 3, half // 2, edge), low),
        pltpu.VMEM((2, 3, half // 2, edge), low),
        pltpu.VMEM((2, 3, half // 2, edge), low),
        pltpu.VMEM((4, edge, edge), low),
        pltpu.VMEM((4 * listed, edge), wide),
        pltpu.VMEM((3, listed, edge), wide),
        pltpu.VMEM((listed, edge), wide),
        pltpu.VMEM((edge, 2 * edge), low),
        pltpu.SMEM(ids.shape, jnp.int32),
        dma(2 + len(given) + listed + depth + 1),
        dma(3, depth),
        dma(3, depth),
        dma(depth),
        dma(depth),
        dma(2 * depth),
        dma(2 * depth),
        dma(4),
        dma(4),
        dma(3),
        dma(3),
        dma(3),
        dma(3),
        dma(2, 2),
        dma(2, 2),
        dma(2, 2),
        dma(2, 2),
        dma(2),
        dma(2),
        dma(2),
        dma(2),
        dma(4),
        dma(4),
    ]
    final, refined = pl.pallas_call(
        quarter_kernel,
        in_specs=[any_space] * (5 + len(given)),
        out_specs=[vmem, vmem],
        out_shape=[
            jax.ShapeDtypeStruct((3, edge, edge), low),
            jax.ShapeDtypeStruct((edge, edge), low),
        ],
        scratch_shapes=scratch,
        compiler_params=pltpu.CompilerParams(
            vmem_limit_bytes=60 * 1024 * 1024, collective_id=0, has_side_effects=True
        ),
        cost_estimate=pl.CostEstimate(flops=12000000000, bytes_accessed=12000000, transcendentals=0),
    )(ids, micrograph, search, library, ctf, *given)
    number = float(lax.axis_size("orient") * search.shape[0])
    block = lambda: pl.BlockSpec((edge // 3, edge), lambda i: (i, 0))
    return tuple(
        pl.pallas_call(
            functools.partial(finish_kernel, number),
            grid=(3,),
            in_specs=[pl.BlockSpec((3, edge // 3, edge), lambda i: (0, i, 0)), block()],
            out_specs=[block()] * 4,
            out_shape=[jax.ShapeDtypeStruct((edge, edge), wide)] * 4,
        )(final, refined)
    )


def body(micrograph, search_spectra, refine_spectra, ctf, ref_owner, ref_slot):
    edge = micrograph.shape[1]
    if quartered(search_spectra, refine_spectra, edge):
        return quarter_maps(micrograph, search_spectra, refine_spectra[0], ctf, ref_owner, ref_slot)
    half = edge // 2
    fwd_cos, fwd_sin, inv_cos, inv_sin = make_tables(edge)
    ctf_gain = jnp.concatenate([ctf, ctf], 1)
    rows_owned = search_spectra.shape[1]
    first_row = lax.axis_index("mic") * rows_owned
    own_gain = lax.dynamic_slice_in_dim(ctf_gain, first_row, rows_owned, 0)
    filtered = (search_spectra.astype(jnp.float32) * own_gain).astype(jnp.bfloat16)
    folded = fold_half(filtered)
    spectrum = forward(micrograph, fwd_cos, fwd_sin)

    library = refine_spectra[0]
    block_size = library.shape[0]
    ids = lax.all_gather(ref_owner[:, 0] * block_size + ref_slot[:, 0], "orient", axis=0, tiled=True)
    slots = lax.axis_index("orient") * block_size + jnp.arange(block_size, dtype=jnp.int32)
    wanted = jnp.any(slots[:, None] == ids[None, :], axis=1).astype(jnp.int32)
    cs = jnp.asarray(np.concatenate([inv_cos, inv_sin], 1))

    spec = spectrum.astype(jnp.float32)
    g_r, g_i = spec[:, :edge], spec[:, edge:]
    dc = jnp.stack([g_r[:, 0], g_i[:, 0]], 1)
    ny = jnp.stack([g_r[:, half], g_i[:, half]], 1)
    ga = (dc - ny) * 0.5
    gb = (dc + ny) * 0.5
    lane = lax.broadcasted_iota(jnp.int32, (edge, half), 1)
    h_r = jnp.where(lane == 0, ga[:, 0:1], g_r[:, :half])
    h_i = jnp.where(lane == 0, ga[:, 1:2], g_i[:, :half])
    gr = jnp.concatenate([h_r, h_r], 1)
    gi = jnp.concatenate([h_i, h_i], 1)
    sin_rows = -inv_sin[:half]
    sin_rows[0] = inv_cos[half]
    col = jnp.asarray(np.concatenate([inv_cos[:half], sin_rows], 0))
    peak, total, square, refined = all_maps(
        folded, gr, gi, gb, cs, col, library, ctf, spectrum, wanted
    )
    count = float(lax.axis_size("orient") * search_spectra.shape[0])
    return (peak, total / count, peak * lax.rsqrt(square / count + 1e-05), refined)


def solution(mesh):
    in_specs = (
        P("mic", None),
        P("orient", "mic", None),
        P("mic", "orient", None, None),
        P(),
        P(("mic", "orient"), None),
        P(("mic", "orient"), None),
    )
    out_specs = (P("mic", None), P("mic", None), P("mic", None), P("mic", None))
    return jax.shard_map(body, mesh=mesh, in_specs=in_specs, out_specs=out_specs, check_vma=False)
```

```python
import functools
import math

import jax
import jax.numpy as jnp
import numpy as np
from jax import lax
from jax.experimental import pallas as pl
from jax.experimental.pallas import tpu as pltpu
from jax.sharding import PartitionSpec as P

MESH = pl.DeviceIdType.MESH
LOW = -3.0e38


def make_tables(box_edge):
    positions = np.arange(box_edge, dtype=np.int32)
    products = positions[:, None] * positions[None, :] % box_edge
    angles = products.astype(np.float32) * np.float32(2.0 * math.pi / box_edge)
    cosine = np.cos(angles)
    sines = np.sin(angles)
    narrow = lambda a: a.astype(np.float32).astype(jnp.bfloat16)
    fwd_cos, fwd_sin = narrow(cosine), narrow(sines)
    inv_cos = narrow(cosine / np.float32(box_edge))
    inv_sin = narrow(sines / np.float32(box_edge))
    return (fwd_cos, fwd_sin, inv_cos, inv_sin)


def forward(tile_image, fwd_cos, fwd_sin):
    box_edge = tile_image.shape[0]
    full_map = jnp.asarray(np.concatenate([fwd_cos, fwd_sin], 1))
    halved = jnp.dot(tile_image, full_map, preferred_element_type=jnp.float32).astype(jnp.bfloat16)
    ar, ai = halved[:, :box_edge], -halved[:, box_edge:]
    stacked = jnp.concatenate(
        [jnp.concatenate([ar, ai], 1), jnp.concatenate([ai, -ar], 1)], 0
    )
    return jnp.dot(full_map, stacked, preferred_element_type=jnp.float32).astype(jnp.bfloat16)


def fold_matrices(edge):
    half = edge // 2
    mirror = np.zeros((2 * edge, edge), np.float32)
    for l in range(1, half):
        mirror[edge - l, l] = 1.0
        mirror[2 * edge - l, half + l] = -1.0
    mirror[0, 0], mirror[edge + half, 0] = 0.5, 0.5
    mirror[edge, half], mirror[half, half] = -0.5, 0.5
    row = lax.broadcasted_iota(jnp.int32, (2 * edge, edge), 0)
    col = lax.broadcasted_iota(jnp.int32, (2 * edge, edge), 1)
    own = jnp.where(row == jnp.where(col < half, col, col + half), 1.0, 0.0)
    first = jnp.where(row == 0, 0.5, jnp.where(row == edge + half, -0.5, 0.0))
    middle = jnp.where((row == edge) | (row == half), 0.5, 0.0)
    own = jnp.where(col == 0, first, jnp.where(col == half, middle, own))
    return own.astype(jnp.bfloat16), jnp.asarray(mirror, jnp.bfloat16)


def fold_half(filtered):
    count, rows, width = filtered.shape
    edge = width // 2
    mics = lax.axis_size("mic")
    own_map, mirror_map = fold_matrices(edge)
    mirrored = jnp.einsum(
        "tkc,cl->tkl", filtered, mirror_map, preferred_element_type=jnp.float32
    ).astype(jnp.bfloat16)
    flip = np.zeros((rows, rows), np.float32)
    for i in range(1, rows):
        flip[i, rows - i] = 1.0
    turned = jnp.einsum(
        "ik,tkl->til", jnp.asarray(flip, jnp.bfloat16), mirrored, preferred_element_type=jnp.float32
    ).astype(jnp.bfloat16)
    first = lax.ppermute(mirrored[:, 0, :], "mic", [(m, (mics - m) % mics) for m in range(mics)])
    rest = lax.ppermute(turned, "mic", [(m, mics - 1 - m) for m in range(mics)])
    own = jnp.einsum("tkc,cl->tkl", filtered, own_map, preferred_element_type=jnp.float32)
    row = lax.broadcasted_iota(jnp.int32, (1, rows, 1), 1)
    other = jnp.where(row == 0, first[:, None, :].astype(jnp.float32), rest.astype(jnp.float32))
    return (own + other).astype(jnp.bfloat16)


def correlate(e, gr_ref, gi_ref, gb_ref, cs_ref, col_ref, flip_ref):
    edge = gr_ref.shape[0]
    half = edge // 2
    es = jnp.concatenate([e[:, half:], e[:, :half]], axis=1)
    gr = gr_ref[...]
    gi = gi_ref[...]
    lane = lax.broadcasted_iota(jnp.int32, (edge, edge), 1)
    low = lane < half
    narrow = lax.broadcasted_iota(jnp.int32, (edge, 128), 1)
    dr = jnp.dot(
        flip_ref[...],
        jnp.where(narrow == 0, e[:, :128], pltpu.roll(es[:, :128], 1, 1)).astype(jnp.bfloat16),
        preferred_element_type=jnp.float32,
    )
    gbr, gbi = gb_ref[:, 0:1], gb_ref[:, 1:2]
    mr, mi = dr[:, 0:1], dr[:, 1:2]
    fix_r = gbr * mr - gbi * mi
    fix_i = gbr * mi + gbi * mr
    ge, ges = gr * e, gr * es
    he, hes = gi * e, gi * es
    top = jnp.where(low, ge, -ge) + hes
    bottom = ges + jnp.where(low, -he, he)
    at_r, at_i = lane == 0, lane == half
    top = top + jnp.where(at_r, fix_r, jnp.where(at_i, fix_i, 0.0))
    bottom = bottom + jnp.where(at_r, -fix_i, jnp.where(at_i, fix_r, 0.0))
    stacked = jnp.concatenate([top.astype(jnp.bfloat16), bottom.astype(jnp.bfloat16)], axis=0)
    v = jnp.dot(cs_ref[...], stacked, preferred_element_type=jnp.float32).astype(jnp.bfloat16)
    return jnp.dot(v, col_ref[...], preferred_element_type=jnp.float32)


def accumulate(corr, peak_ref, total_ref, square_ref):
    peak_ref[...] = jnp.maximum(peak_ref[...], corr)
    total_ref[...] += corr
    square_ref[...] += corr * corr


def clear(peak_ref, total_ref, square_ref):
    peak_ref[...] = jnp.full(peak_ref.shape, -3.0e38, jnp.float32)
    total_ref[...] = jnp.zeros(total_ref.shape, jnp.float32)
    square_ref[...] = jnp.zeros(square_ref.shape, jnp.float32)


def refine_correlation(template, ctf_ref, g_ref, cs_ref):
    edge = ctf_ref.shape[0]
    gain = ctf_ref[...]
    narrow = lambda a: a.astype(jnp.bfloat16)
    fr = narrow(template[:, :edge].astype(jnp.float32) * gain).astype(jnp.float32)
    fi = narrow(template[:, edge:].astype(jnp.float32) * gain).astype(jnp.float32)
    gr = g_ref[:, :edge].astype(jnp.float32)
    gi = g_ref[:, edge:].astype(jnp.float32)
    zr = narrow(gr * fr + gi * fi)
    zi = narrow(gi * fr - gr * fi)
    ci, si = cs_ref[:, :edge], cs_ref[:, edge:]
    dot = lambda a, b: jnp.dot(a, b, preferred_element_type=jnp.float32)
    ur = narrow(dot(ci, zr) - dot(si, zi))
    ui = narrow(dot(si, zr) + dot(ci, zi))
    return dot(ur, ci) - dot(ui, si)


def search_kernel(e_ref, *refs):
    @pl.when(pl.program_id(0) == 0)
    def _():
        clear(*refs[6:])

    edge = refs[0].shape[0]
    e = e_ref[...].reshape(edge, edge).astype(jnp.float32)
    accumulate(correlate(e, *refs[:6]), *refs[6:])


def all_maps(folded, gr, gi, gb, cs, col, library, ctf, spectrum, wanted):
    count, rows, edge = folded.shape
    place = lambda axis: lax.broadcasted_iota(jnp.int32, (edge, edge), axis)
    flip = ((place(0) + place(1)) % edge == 0).astype(jnp.bfloat16)
    whole = lambda a: pl.BlockSpec(a.shape, lambda t: (0, 0))
    out = jax.ShapeDtypeStruct((edge, edge), jnp.float32)
    cost = pl.CostEstimate(
        flops=count * 350000000, bytes_accessed=count * 600000, transcendentals=0
    )
    refined = refine_map(library, ctf, spectrum, cs, wanted)
    gathered = lax.all_gather(folded, "mic", axis=1, tiled=True)[None]
    maps = pl.pallas_call(
        search_kernel,
        grid=(count,),
        in_specs=[pl.BlockSpec((1, 1, edge, edge), lambda t: (0, t, 0, 0))]
        + [whole(a) for a in (gr, gi, gb, cs, col, flip)],
        out_specs=[pl.BlockSpec((edge, edge), lambda t: (0, 0))] * 3,
        out_shape=[out] * 3,
        compiler_params=pltpu.CompilerParams(vmem_limit_bytes=40 * 1024 * 1024),
        cost_estimate=cost,
    )(gathered, gr, gi, gb, cs, col, flip)
    return merge([*maps, refined])


def refine_kernel(lib_ref, ctf_ref, g_ref, cs_ref, wanted_ref, out_ref):
    step = pl.program_id(0)
    edge = ctf_ref.shape[0]

    @pl.when(step == 0)
    def _():
        out_ref[...] = jnp.full((edge, edge), -3.0e38, jnp.float32)

    @pl.when(wanted_ref[step] > 0)
    def _():
        corr = refine_correlation(lib_ref[0], ctf_ref, g_ref, cs_ref)
        out_ref[...] = jnp.maximum(out_ref[...], corr)


def refine_map(library, ctf, spectrum, cs, wanted):
    count, edge, width = library.shape
    whole = lambda a: pl.BlockSpec(a.shape, lambda t: (0, 0))
    return pl.pallas_call(
        refine_kernel,
        grid=(count,),
        in_specs=[pl.BlockSpec((1, edge, width), lambda t: (t, 0, 0))]
        + [whole(a) for a in (ctf, spectrum, cs)]
        + [pl.BlockSpec(memory_space=pltpu.SMEM)],
        out_specs=pl.BlockSpec((edge, edge), lambda t: (0, 0)),
        out_shape=jax.ShapeDtypeStruct((edge, edge), jnp.float32),
        compiler_params=pltpu.CompilerParams(vmem_limit_bytes=40 * 1024 * 1024),
        cost_estimate=pl.CostEstimate(flops=count * 700000000, bytes_accessed=count * 1200000, transcendentals=0),
    )(library, ctf, spectrum, cs, wanted)


def join(left, right):
    right = [a.astype(jnp.float32) for a in right]
    return [
        jnp.maximum(a, b) if i in (0, 3) else a + b for i, (a, b) in enumerate(zip(left, right))
    ]


def merge(maps):
    size = lax.axis_size("orient")
    edge = maps[0].shape[0]
    half = edge // 2
    core = lax.axis_index("orient") % 2
    near = [(i, i ^ 1) for i in range(size)]
    narrow = lambda values: [a.astype(jnp.bfloat16) for a in values]
    mine = [lax.dynamic_slice_in_dim(a, core * half, half, 0) for a in maps]
    theirs = narrow(lax.dynamic_slice_in_dim(a, (1 - core) * half, half, 0) for a in maps)
    state = join(mine, lax.ppermute(jnp.stack(theirs), "orient", near))
    distance = 2
    while distance < size:
        far = [(i, i ^ distance) for i in range(size)]
        state = join(state, lax.ppermute(jnp.stack(narrow(state)), "orient", far))
        distance *= 2
    final = jnp.stack(narrow(state))
    other = lax.ppermute(final, "orient", near)
    first = jnp.where(core == 0, final, other)
    second = jnp.where(core == 0, other, final)
    return [jnp.concatenate([first[i], second[i]], 0).astype(jnp.float32) for i in range(len(maps))]


def quartered(search, library, edge):
    sizes = (lax.axis_size("mic"), lax.axis_size("orient"))
    return sizes == (8, 4) and edge == 384 and search.shape[:2] == (16, 48)


def column_plan(edge):
    half, lanes = edge // 2, 128
    plan = [("re", l) for l in range(half)]
    plan += [("im", l) for l in range(lanes, half)]
    return plan + [("im", l) for l in range(lanes)]


def quarter_tables(edge):
    half, slab, lanes = edge // 2, edge // 4, 128
    fwd_cos, fwd_sin, inv_cos, inv_sin = make_tables(edge)
    plan = column_plan(edge)
    packed = plan.index(("im", 0))
    own = np.zeros((2 * edge, edge), np.float32)
    mirror = np.zeros((2 * edge, edge), np.float32)
    freq, sign = [], []
    col = np.zeros((edge, edge), np.float32)
    for place, (kind, l) in enumerate(plan):
        freq.append(half if place == packed else l)
        sign.append(-1.0 if kind == "im" and place != packed else 1.0)
        if kind == "re":
            col[place] = inv_cos[l]
        else:
            col[place] = inv_cos[half] if place == packed else -inv_sin[l].astype(np.float32)
        if l == 0:
            continue
        if kind == "re":
            own[l, place] = 1.0
            mirror[edge - l, place] = 1.0
        else:
            own[edge + l, place] = 1.0
            mirror[2 * edge - l, place] = -1.0
    own[0, 0], own[edge + half, 0] = 0.5, -0.5
    own[edge, packed], own[half, packed] = 0.5, 0.5
    mirror[0, 0], mirror[edge + half, 0] = 0.5, 0.5
    mirror[edge, packed], mirror[half, packed] = -0.5, 0.5
    order = np.concatenate([np.arange(s * slab, (s + 1) * slab) for s in (0, 3, 1, 2)])
    flips = np.zeros((2, half + 16, half), np.float32)
    for pair, moved in enumerate((slab, 0)):
        for u in range(half):
            flips[pair, half if u == moved else u, (half - u) % half] = 1.0
    turn = np.zeros((edge, edge), np.float32)
    for i, k in enumerate(order):
        turn[i, list(order).index((edge - k) % edge)] = 1.0
    low = lambda a: jnp.asarray(np.asarray(a, np.float32), jnp.bfloat16)
    side = lambda a, b: low(np.concatenate([np.asarray(a, np.float32), np.asarray(b, np.float32)], 1))
    return dict(
        cs=side(inv_cos, inv_sin),
        cs_turned=side(inv_cos[:, order], inv_sin[:, order]),
        col=low(col),
        fold=side(own, mirror),
        flips=low(flips),
        turn=low(turn),
        full=side(fwd_cos, fwd_sin),
        full_cols=side(fwd_cos[:, freq], fwd_sin[:, freq]),
        full_rows=side(fwd_cos[order], fwd_sin[order]),
        sign=jnp.asarray(np.tile(np.asarray(sign, np.float32)[None], (8, 1))),
    )


TABLES = ("cs", "cs_turned", "col", "fold", "flips", "turn", "full", "full_cols", "full_rows", "sign")


def dot(a, b):
    return jnp.dot(a, b, preferred_element_type=jnp.float32)


def spectrum_of(image, columns, rows):
    edge = image.shape[0]
    halved = dot(image, columns).astype(jnp.bfloat16)
    ar, ai = halved[:, :edge], -halved[:, edge:]
    stacked = jnp.concatenate(
        [jnp.concatenate([ar, ai], 1), jnp.concatenate([ai, -ar], 1)], 0
    )
    return dot(rows, stacked).astype(jnp.bfloat16)


def quarter_kernel(ids_in, image_in, search_in, library_in, ctf_in, *refs):
    inputs, refs = refs[: len(TABLES)], refs[len(TABLES) :]
    final, refined = refs[:2]
    tables, refs = refs[2 : 2 + len(TABLES)], refs[2 + len(TABLES) :]
    tab = dict(zip(TABLES, tables))
    (image, library, ctf, images, raw, folded, gains, pair_e, stack, maps, refmap,
     x_out, x_in, y_out, y_in, z_out, z_in, shared, mask_out, mask_in, cap, g_own,
     ids_ref, block_in, sums, sum_raw, sum_e) = refs[:27]
    (load_sem, raw_s, raw_r, ez_s, ez_r, ec_s, ec_r, im_s, im_r, mk_s, mk_r, sh_s, sh_r,
     x_s, x_r, y_s, y_r, z_s, z_r, ag_s, ag_r, co_s, co_r, su_s, su_r, sr_s, sr_r, sx_s, sx_r) = refs[27:]
    edge = ctf.shape[0]
    half, slab, rows = edge // 2, edge // 4, raw.shape[1] // 4
    depth = raw.shape[0]
    listed = library.shape[0]
    me, block = lax.axis_index("mic"), lax.axis_index("orient")
    z, x = me // 2, me % 2
    y, c = block // 2, block % 2
    zm, xm, ym, cm = 3 - z, 1 - x, 1 - y, 1 - c
    zn = z + 1 - 2 * (z % 2)
    upper = z // 2
    outer = (z + 1) % 4 // 2
    home = c == x
    away = c != x
    place = lambda z, x, y, c: {"mic": z * 2 + x, "orient": y * 2 + c}
    trio = [(z, xm), (zm, x), (zm, xm)]
    peers = [(y, cm), (ym, c), (ym, cm)]
    partners = [place(a, b, y, c) for a, b in trio] + [place(z, x, a, b) for a, b in peers]
    partners.append(place(zn, x, y, c))

    barrier = pltpu.get_barrier_semaphore()
    for partner in partners:
        pl.semaphore_signal(barrier, inc=1, device_id=partner, device_id_type=MESH)

    def spot(zz, xx):
        return pl.ds(pl.multiple_of(zz // 2 * slab + xx * rows, 16), rows)

    loads = [
        pltpu.make_async_copy(image_in, image, load_sem.at[0]),
        pltpu.make_async_copy(ctf_in, ctf, load_sem.at[1]),
    ]
    for i, (a, b) in enumerate(zip(inputs, tables)):
        loads.append(pltpu.make_async_copy(a, b, load_sem.at[2 + i]))
    count = len(loads)
    lib_loads = [
        pltpu.make_async_copy(library_in.at[j], library.at[j], load_sem.at[count + j])
        for j in range(listed)
    ]
    count += listed
    own_loads = [
        pltpu.make_async_copy(
            search_in.at[x * 2 * depth + upper * depth + j],
            raw.at[j, spot(z, x)],
            load_sem.at[count + j],
        )
        for j in range(depth)
    ]
    named = [pltpu.make_async_copy(ids_in, ids_ref, load_sem.at[count + depth])]
    block_load = pltpu.make_async_copy(search_in, block_in, load_sem.at[count + depth + 1])
    block_load.start()
    for load in named + loads + lib_loads + own_loads:
        load.start()
    for load in named:
        load.wait()

    row = lax.broadcasted_iota(jnp.int32, mask_out.shape, 0)
    mask = jnp.zeros(mask_out.shape, jnp.float32)
    for entry in range(ids_ref.shape[1]):
        mask = jnp.where(row == ids_ref[0, entry], 1.0, mask)
    mask_out[...] = mask

    def remote(src, dst, send, recv, target):
        return pltpu.make_async_remote_copy(
            src_ref=src, dst_ref=dst, send_sem=send, recv_sem=recv, device_id=target, device_id_type=MESH
        )

    def send_raw(q, j):
        zz, xx = trio[q]
        return remote(
            search_in.at[xx * 2 * depth + zz // 2 * depth + j],
            raw.at[j, spot(z, x)],
            raw_s.at[q, j],
            raw_r.at[q, j],
            place(zz, xx, y, c),
        )

    def take_raw(q, j):
        zz, xx = trio[q]
        spots = raw.at[j, spot(zz, xx)]
        return remote(spots, spots, raw_s.at[q, j], raw_r.at[q, j], place(zz, xx, y, c))

    beside, across = place(z, xm, y, c), place(zm, x, y, c)
    send_own = remote(image_in, images.at[0], im_s.at[0], im_r.at[0], beside)
    mine = pl.ds(pl.multiple_of(y * half, 16), half)
    theirs = pl.ds(pl.multiple_of(ym * half, 16), half)
    twin = place(z, x, ym, c)
    core = place(z, x, y, cm)
    send_far = remote(image_in.at[mine], images.at[1, mine], im_s.at[1], im_r.at[1], across)
    pass_far = remote(images.at[1, mine], images.at[1, mine], im_s.at[2], im_r.at[2], beside)
    pass_twin = remote(images.at[1, mine], images.at[1, mine], im_s.at[3], im_r.at[3], twin)
    take_twin = remote(images.at[1, theirs], images.at[1, theirs], im_s.at[3], im_r.at[3], twin)

    def send_mask(q):
        yy, cc = peers[q]
        part = mask_out.at[pl.ds(pl.multiple_of((yy * 2 + cc) * listed, 8), listed)]
        return remote(part, mask_in.at[q], mk_s.at[q], mk_r.at[q], place(z, x, yy, cc))

    part_c = pl.ds(pl.multiple_of(c * half, 16), half)
    part_o = pl.ds(pl.multiple_of(cm * half, 16), half)
    share_core = remote(shared.at[0], shared.at[1], sh_s.at[0], sh_r.at[0], core)
    share_twin = remote(shared.at[2, part_c], shared.at[3, part_c], sh_s.at[1], sh_r.at[1], twin)
    share_last = remote(refined.at[part_c], refined.at[part_c], sh_s.at[2], sh_r.at[2], core)
    take_last = remote(refined.at[part_o], refined.at[part_o], sh_s.at[2], sh_r.at[2], core)

    def send_sum(q):
        yy, cc = peers[q]
        return remote(sums.at[0], sums.at[q + 1], su_s.at[q], su_r.at[q], place(z, x, yy, cc))

    def sum_part(slot, zz, xx, target):
        rows_of = sum_raw.at[c, spot(zz, xx)]
        return remote(rows_of, rows_of, sr_s.at[slot], sr_r.at[slot], target)

    sum_core = remote(sum_raw.at[c], sum_raw.at[c], sx_s.at[0], sx_r.at[0], core)
    sum_core_take = remote(sum_raw.at[cm], sum_raw.at[cm], sx_s.at[0], sx_r.at[0], core)
    sum_give = remote(sum_e.at[outer], sum_e.at[outer], sx_s.at[1], sx_r.at[1], place(zn, x, y, c))
    sum_take = remote(sum_e.at[1 - outer], sum_e.at[1 - outer], sx_s.at[1], sx_r.at[1], place(zn, x, y, c))
    total_core = remote(final.at[2], final.at[2], co_s.at[4], co_r.at[4], core)

    def send_e(j):
        part = folded.at[c, j, outer]
        return remote(part, part, ez_s.at[j], ez_r.at[j], place(zn, x, y, c))

    def take_e(j):
        part = folded.at[c, j, 1 - outer]
        return remote(part, part, ez_s.at[j], ez_r.at[j], place(zn, x, y, c))

    def core_e(j, source, pair):
        part = folded.at[source, j, pair]
        slot = pair * depth + j
        return remote(part, part, ec_s.at[slot], ec_r.at[slot], place(z, x, y, cm))

    pl.semaphore_wait(barrier, len(partners))
    for q in range(3):
        send_mask(q).start()
    pl.when(home)(lambda: send_far.start())
    for q in (1, 2, 0):
        send_raw(q, 0).start()
    pl.when(home)(lambda: send_own.start())

    refmap[...] = jnp.full(refmap.shape, LOW, jnp.float32)
    for t in range(2):
        maps[t, 0] = jnp.full((edge, edge), LOW, jnp.float32)
        maps[t, 1] = jnp.zeros((edge, edge), jnp.float32)
    for load in loads:
        load.wait()
    block_load.wait()
    own_gain = ctf[pl.ds(pl.multiple_of(me * rows, 8), rows), :]
    own_gain = jnp.concatenate([own_gain, own_gain], 1)

    def add_one(t, acc):
        scaled = (block_in[t].astype(jnp.float32) * own_gain).astype(jnp.bfloat16)
        return acc + scaled.astype(jnp.float32)

    acc = lax.fori_loop(0, block_in.shape[0], add_one, jnp.zeros(own_gain.shape, jnp.float32))
    sums[0] = acc.astype(jnp.bfloat16)
    for q in range(3):
        send_sum(q).start()
    g_own[...] = spectrum_of(image[...], tab["full"][...], tab["full"][...])
    wanted = mask_out[pl.ds(pl.multiple_of(block * listed, 8), listed), :]
    for q in range(3):
        send_mask(q).wait_recv()
        wanted = jnp.maximum(wanted, mask_in[q])
    cap[...] = jnp.where(wanted > 0.0, -LOW, LOW)
    for load in lib_loads:
        load.wait()

    def refine_some(first, last):
        def one(j, carry):
            corr = refine_correlation(library[j], ctf, g_own, tab["cs"])
            refmap[...] = jnp.maximum(refmap[...], jnp.minimum(corr, cap[pl.ds(j, 1), :]))
            return carry

        lax.fori_loop(first, last, one, 0)

    def gain_of(t, picture):
        spec = spectrum_of(picture, tab["full_cols"][...], tab["full_rows"][...]).astype(jnp.float32)
        gr, gi, sign = spec[:, :edge], spec[:, edge:], tab["sign"][0:1, :]
        gains[t, 0] = gr * sign
        gains[t, 1] = gi
        gains[t, 2] = gr
        gains[t, 3] = -gi * sign

    def fold_into(target, filtered):
        both = dot(filtered, tab["fold"][...])
        turned = dot(tab["flips"][outer], both[:, edge:].astype(jnp.bfloat16))
        target[0:half, :] = (both[:, :edge] + turned[0:half]).astype(jnp.bfloat16)
        target[half : half + 16, :] = turned[half:].astype(jnp.bfloat16)

    def fold(j):
        for q in range(3):
            take_raw(q, j).wait_recv()
        own_loads[j].wait()
        near = ctf[pl.ds(pl.multiple_of(outer * slab, 8), slab), :]
        far = ctf[pl.ds(pl.multiple_of((3 - outer) * slab, 8), slab), :]
        gain = jnp.concatenate([near, far], 0)
        gain = jnp.concatenate([gain, gain], 1)
        filtered = (raw[j].astype(jnp.float32) * gain).astype(jnp.bfloat16)
        fold_into(folded.at[c, j, outer], filtered)
        send_e(j).start()
        if j + 2 < depth:
            for q in (1, 2, 0):
                send_raw(q, j).wait_send()
                send_raw(q, j + 2).start()
        core_e(j, c, outer).start()

    def prepare_one(source, held):
        parts = [held[p].astype(jnp.float32) for p in range(2)]
        e = jnp.concatenate(
            [
                parts[0][0:slab],
                parts[0][slab : slab + 16] + parts[1][half:],
                parts[0][slab + 16 : half],
                parts[1][0:16] + parts[0][half:],
                parts[1][16:half],
            ],
            0,
        )
        t0, t1, t2 = e[:, 0:128], e[:, 128:256], e[:, 256:384]
        back = dot(tab["turn"][...], jnp.concatenate([t0, t2], 1).astype(jnp.bfloat16))
        m0, m2 = back[:, 0:128], back[:, 128:256]
        first = lax.broadcasted_iota(jnp.int32, t0.shape, 1) == 0
        pair_e[source, 0, :, 0:128] = jnp.where(first, 0.5 * (t0 + m0), t0)
        pair_e[source, 0, :, 128:256] = t1
        pair_e[source, 0, :, 256:384] = jnp.where(first, 0.5 * (t2 + m2), t2)
        pair_e[source, 1, :, 0:128] = jnp.where(first, 0.5 * (t2 - m2), t2)
        pair_e[source, 1, :, 128:256] = pltpu.roll(t1, 64, 1)
        pair_e[source, 1, :, 256:384] = jnp.where(first, 0.5 * (m0 - t0), t0)

    def prepare(j):
        prepare_one(0, folded.at[0, j])
        prepare_one(1, folded.at[1, j])

    def search(t):
        for n in range(2):
            e, es = pair_e[n, 0], pair_e[n, 1]
            stack[0:edge, n * edge : (n + 1) * edge] = (gains[t, 0] * e + gains[t, 1] * es).astype(jnp.bfloat16)
            stack[edge:, n * edge : (n + 1) * edge] = (gains[t, 2] * es + gains[t, 3] * e).astype(jnp.bfloat16)
        v = dot(tab["cs_turned"][...], stack[...]).astype(jnp.bfloat16)
        one = dot(v[:, 0:edge], tab["col"][...])
        two = dot(v[:, edge:], tab["col"][...])
        maps[t, 0] = jnp.maximum(maps[t, 0], jnp.maximum(one, two))
        maps[t, 1] += one * one + two * two

    def total_map():
        prepare_one(0, sum_e)
        e, es = pair_e[0, 0], pair_e[0, 1]
        stack[0:edge, 0:edge] = (gains[0, 0] * e + gains[0, 1] * es).astype(jnp.bfloat16)
        stack[edge:, 0:edge] = (gains[0, 2] * es + gains[0, 3] * e).astype(jnp.bfloat16)
        v = dot(tab["cs_turned"][...], stack[:, 0:edge]).astype(jnp.bfloat16)
        final[2] = dot(v, tab["col"][...]).astype(jnp.bfloat16)

    def await_core(j):
        core_e(j, cm, outer).wait_recv()
        core_e(j, cm, 1 - outer).wait_recv()

    def templates(j):
        await_core(j)
        prepare(j)

        def one(t, carry):
            search(t)
            return carry

        lax.fori_loop(0, 2, one, 0)

    def arrive(j):
        take_e(j).wait_recv()
        core_e(j, c, 1 - outer).start()

    eighth = lambda n: listed * n // 8
    refine_some(0, eighth(1))

    @pl.when(home)
    def _():
        send_far.wait_recv()
        pass_far.start()
        pass_twin.start()
        images[0] = image[...]

    acc = sums[0].astype(jnp.float32)
    for q in range(3):
        send_sum(q).wait_recv()
        acc = acc + sums[q + 1].astype(jnp.float32)
    sum_raw[c, spot(z, x)] = jnp.where(c == 0, acc[:, :edge], acc[:, edge:]).astype(jnp.bfloat16)
    sum_part(1, z, x, across).start()
    sum_part(0, z, x, beside).start()
    for q in (1, 2, 0):
        send_raw(q, 1).start()
    refine_some(eighth(1), eighth(3))
    fold(0)
    sum_part(1, zm, x, across).wait_recv()
    sum_part(2, zm, x, beside).start()

    @pl.when(away)
    def _():
        pass_far.wait_recv()
        pass_twin.start()
        send_own.wait_recv()

    gain_of(0, images[0])
    refine_some(eighth(3), eighth(5))
    fold(1)
    arrive(0)
    take_twin.wait_recv()
    gain_of(1, images[1])
    templates(0)
    sum_part(0, z, xm, beside).wait_recv()
    sum_part(2, zm, xm, beside).wait_recv()

    @pl.when(away)
    def _():
        sum_core.start()

    arrive(1)
    fold(2)

    @pl.when(home)
    def _():
        sum_core_take.wait_recv()
        fold_into(sum_e.at[outer], jnp.concatenate([sum_raw[0], sum_raw[1]], 1))
        sum_give.start()

    templates(1)
    refine_some(eighth(5), listed)
    shared[0] = refmap[...].astype(jnp.bfloat16)
    share_core.start()
    fold(3)
    arrive(2)

    @pl.when(home)
    def _():
        sum_take.wait_recv()
        total_map()
        total_core.start()

    share_core.wait_recv()
    shared[2] = jnp.maximum(shared[0], shared[1])
    share_twin.start()
    templates(2)
    arrive(3)
    share_twin.wait_recv()
    refined[part_c] = jnp.maximum(shared[2, part_c], shared[3, part_c])
    share_last.start()
    await_core(3)
    prepare(3)

    quarter = half // 2
    keep = [pl.ds(pl.multiple_of(a * half + y * quarter, 16), quarter) for a in range(2)]
    give = [pl.ds(pl.multiple_of(a * half + ym * quarter, 16), quarter) for a in range(2)]
    upper_rows = slice(0, half)

    def x_send(t, part):
        rows = pl.ds(0, half) if part == 0 else keep[1]
        return remote(x_out.at[t, :, rows], x_in.at[t, :, rows], x_s.at[t, part], x_r.at[t, part], beside)

    def y_send(t, part):
        return remote(y_out.at[t, part], y_in.at[t, part], y_s.at[t, part], y_r.at[t, part], twin)

    def z_send(part):
        return remote(z_out.at[part], z_in.at[part], z_s.at[part], z_r.at[part], across)

    def final_send(part):
        return remote(final.at[0:2, keep[part]], final.at[0:2, keep[part]], ag_s.at[part], ag_r.at[part], twin)

    def final_take(part):
        return remote(final.at[0:2, give[part]], final.at[0:2, give[part]], ag_s.at[part], ag_r.at[part], twin)

    def core_final(part, where):
        rows = (keep, give)[where][part]
        slot = where * 2 + part
        return remote(final.at[0:2, rows], final.at[0:2, rows], co_s.at[slot], co_r.at[slot], core)

    def merge_in(t, where, piece):
        maps[t, 0, where] = jnp.maximum(maps[t, 0, where], piece[0].astype(jnp.float32))
        maps[t, 1, where] += piece[1].astype(jnp.float32)

    def start_y(t, part):
        y_out[t, part] = maps[t, :, give[part]].astype(jnp.bfloat16)
        y_send(t, part).start()

    def start_x(t, part):
        rows = upper_rows if part == 0 else keep[1]
        x_out[t, :, rows] = maps[t, :, rows].astype(jnp.bfloat16)
        x_send(t, part).start()

    def start_z(part):
        z_out[part] = maps[1, :, keep[part]].astype(jnp.bfloat16)
        z_send(part).start()

    def relay(t):
        x_send(t, 0).wait_recv()
        merge_in(t, give[0], x_in[t, :, give[0]])
        start_y(t, 0)
        merge_in(t, keep[0], x_in[t, :, keep[0]])

    search(1)
    pl.when(away)(lambda: start_x(1, 0))
    start_y(1, 1)
    search(0)
    pl.when(home)(lambda: relay(1))
    y_send(1, 1).wait_recv()
    merge_in(1, keep[1], y_in[1, 1])

    @pl.when(away)
    def _():
        start_x(1, 1)
        start_x(0, 0)

    start_y(0, 1)

    @pl.when(home)
    def _():
        y_send(1, 0).wait_recv()
        merge_in(1, keep[0], y_in[1, 0])
        start_z(0)
        x_send(1, 1).wait_recv()
        merge_in(1, keep[1], x_in[1, :, keep[1]])
        start_z(1)
        relay(0)

    y_send(0, 1).wait_recv()
    merge_in(0, keep[1], y_in[0, 1])
    pl.when(away)(lambda: start_x(0, 1))

    @pl.when(home)
    def _():
        y_send(0, 0).wait_recv()
        merge_in(0, keep[0], y_in[0, 0])
        x_send(0, 1).wait_recv()
        merge_in(0, keep[1], x_in[0, :, keep[1]])

    @pl.when(home)
    def _():
        for part in range(2):
            z_send(part).wait_recv()
            merge_in(0, keep[part], z_in[part])
            final[0:2, keep[part]] = maps[0, :, keep[part]].astype(jnp.bfloat16)
            final_send(part).start()
            core_final(part, 0).start()
        for part in range(2):
            final_take(part).wait_recv()
            core_final(part, 1).start()
        for part in range(2):
            y_send(0, part).wait_send()
            y_send(1, part).wait_send()
            z_send(part).wait_send()
            final_send(part).wait_send()
            core_final(part, 0).wait_send()
            core_final(part, 1).wait_send()

    @pl.when(away)
    def _():
        sum_core.wait_send()
        total_core.wait_recv()
        for part in range(2):
            x_send(0, part).wait_send()
            x_send(1, part).wait_send()
            y_send(part, 1).wait_send()
        for part in range(2):
            core_final(part, 0).wait_recv()
        for part in range(2):
            core_final(part, 1).wait_recv()

    take_last.wait_recv()
    share_core.wait_send()
    share_twin.wait_send()
    share_last.wait_send()
    pass_twin.wait_send()
    for q in range(3):
        send_mask(q).wait_send()
        send_sum(q).wait_send()
    sum_part(0, z, x, beside).wait_send()
    sum_part(1, z, x, across).wait_send()
    sum_part(2, zm, x, beside).wait_send()
    for j in range(depth):
        for q in range(3):
            if j + 2 >= depth:
                send_raw(q, j).wait_send()
        send_e(j).wait_send()
        core_e(j, c, outer).wait_send()
        core_e(j, c, 1 - outer).wait_send()

    @pl.when(home)
    def _():
        sum_give.wait_send()
        total_core.wait_send()
        send_own.wait_send()
        send_far.wait_send()
        pass_far.wait_send()


def finish_kernel(number, final, best, peak, mean, scaled, refined):
    top = final[0].astype(jnp.float32)
    peak[...] = top
    mean[...] = final[2].astype(jnp.float32) / number
    scaled[...] = top * lax.rsqrt(final[1].astype(jnp.float32) / number + 1e-05)
    refined[...] = best[...].astype(jnp.float32)


def quarter_maps(micrograph, search, library, ctf, ref_owner, ref_slot):
    edge = micrograph.shape[1]
    half, depth, listed = edge // 2, search.shape[0] // 4, library.shape[0]
    ids = (ref_owner * listed + ref_slot).reshape(1, -1)
    tables = quarter_tables(edge)
    given = [tables[name] for name in TABLES]
    any_space = pl.BlockSpec(memory_space=pl.ANY)
    vmem = pl.BlockSpec(memory_space=pltpu.VMEM)
    low, wide = jnp.bfloat16, jnp.float32
    dma = lambda *shape: pltpu.SemaphoreType.DMA(shape)
    scratch = [pltpu.VMEM(a.shape, a.dtype) for a in given]
    scratch += [
        pltpu.VMEM((edge, edge), low),
        pltpu.VMEM(library.shape, low),
        pltpu.VMEM((edge, edge), wide),
        pltpu.VMEM((2, edge, edge), low),
        pltpu.VMEM((depth, half, 2 * edge), low),
        pltpu.VMEM((2, depth, 2, half + 16, edge), low),
        pltpu.VMEM((2, 4, edge, edge), wide),
        pltpu.VMEM((2, 2, edge, edge), wide),
        pltpu.VMEM((2 * edge, 2 * edge), low),
        pltpu.VMEM((2, 2, edge, edge), wide),
        pltpu.VMEM((edge, edge), wide),
        pltpu.VMEM((2, 2, edge, edge), low),
        pltpu.VMEM((2, 2, edge, edge), low),
        pltpu.VMEM((2, 2, 2, half // 2, edge), low),
        pltpu.VMEM((2, 2, 2, half // 2, edge), low),
        pltpu.VMEM((2, 2, half // 2, edge), low),
        pltpu.VMEM((2, 2, half // 2, edge), low),
        pltpu.VMEM((4, edge, edge), low),
        pltpu.VMEM((4 * listed, edge), wide),
        pltpu.VMEM((3, listed, edge), wide),
        pltpu.VMEM((listed, edge), wide),
        pltpu.VMEM((edge, 2 * edge), low),
        pltpu.SMEM(ids.shape, jnp.int32),
        pltpu.VMEM(search.shape, low),
        pltpu.VMEM((4,) + search.shape[1:], low),
        pltpu.VMEM((2, half, edge), low),
        pltpu.VMEM((2, half + 16, edge), low),
        dma(2 + len(given) + listed + depth + 2),
        dma(3, depth),
        dma(3, depth),
        dma(depth),
        dma(depth),
        dma(2 * depth),
        dma(2 * depth),
        dma(4),
        dma(4),
        dma(3),
        dma(3),
        dma(3),
        dma(3),
        dma(2, 2),
        dma(2, 2),
        dma(2, 2),
        dma(2, 2),
        dma(2),
        dma(2),
        dma(2),
        dma(2),
        dma(5),
        dma(5),
        dma(3),
        dma(3),
        dma(3),
        dma(3),
        dma(2),
        dma(2),
    ]
    final, refined = pl.pallas_call(
        quarter_kernel,
        in_specs=[any_space] * (5 + len(given)),
        out_specs=[vmem, vmem],
        out_shape=[
            jax.ShapeDtypeStruct((3, edge, edge), low),
            jax.ShapeDtypeStruct((edge, edge), low),
        ],
        scratch_shapes=scratch,
        compiler_params=pltpu.CompilerParams(
            vmem_limit_bytes=60 * 1024 * 1024, collective_id=0, has_side_effects=True
        ),
        cost_estimate=pl.CostEstimate(flops=12000000000, bytes_accessed=12000000, transcendentals=0),
    )(ids, micrograph, search, library, ctf, *given)
    number = float(lax.axis_size("orient") * search.shape[0])
    block = lambda: pl.BlockSpec((edge, edge), lambda i: (0, 0))
    return tuple(
        pl.pallas_call(
            functools.partial(finish_kernel, number),
            grid=(1,),
            in_specs=[vmem, vmem],
            out_specs=[block()] * 4,
            out_shape=[jax.ShapeDtypeStruct((edge, edge), wide)] * 4,
        )(final, refined)
    )


def body(micrograph, search_spectra, refine_spectra, ctf, ref_owner, ref_slot):
    edge = micrograph.shape[1]
    if quartered(search_spectra, refine_spectra, edge):
        return quarter_maps(micrograph, search_spectra, refine_spectra[0], ctf, ref_owner, ref_slot)
    half = edge // 2
    fwd_cos, fwd_sin, inv_cos, inv_sin = make_tables(edge)
    ctf_gain = jnp.concatenate([ctf, ctf], 1)
    rows_owned = search_spectra.shape[1]
    first_row = lax.axis_index("mic") * rows_owned
    own_gain = lax.dynamic_slice_in_dim(ctf_gain, first_row, rows_owned, 0)
    filtered = (search_spectra.astype(jnp.float32) * own_gain).astype(jnp.bfloat16)
    folded = fold_half(filtered)
    spectrum = forward(micrograph, fwd_cos, fwd_sin)

    library = refine_spectra[0]
    block_size = library.shape[0]
    ids = lax.all_gather(ref_owner[:, 0] * block_size + ref_slot[:, 0], "orient", axis=0, tiled=True)
    slots = lax.axis_index("orient") * block_size + jnp.arange(block_size, dtype=jnp.int32)
    wanted = jnp.any(slots[:, None] == ids[None, :], axis=1).astype(jnp.int32)
    cs = jnp.asarray(np.concatenate([inv_cos, inv_sin], 1))

    spec = spectrum.astype(jnp.float32)
    g_r, g_i = spec[:, :edge], spec[:, edge:]
    dc = jnp.stack([g_r[:, 0], g_i[:, 0]], 1)
    ny = jnp.stack([g_r[:, half], g_i[:, half]], 1)
    ga = (dc - ny) * 0.5
    gb = (dc + ny) * 0.5
    lane = lax.broadcasted_iota(jnp.int32, (edge, half), 1)
    h_r = jnp.where(lane == 0, ga[:, 0:1], g_r[:, :half])
    h_i = jnp.where(lane == 0, ga[:, 1:2], g_i[:, :half])
    gr = jnp.concatenate([h_r, h_r], 1)
    gi = jnp.concatenate([h_i, h_i], 1)
    sin_rows = -inv_sin[:half]
    sin_rows[0] = inv_cos[half]
    col = jnp.asarray(np.concatenate([inv_cos[:half], sin_rows], 0))
    peak, total, square, refined = all_maps(
        folded, gr, gi, gb, cs, col, library, ctf, spectrum, wanted
    )
    count = float(lax.axis_size("orient") * search_spectra.shape[0])
    return (peak, total / count, peak * lax.rsqrt(square / count + 1e-05), refined)


def solution(mesh):
    in_specs = (
        P("mic", None),
        P("orient", "mic", None),
        P("mic", "orient", None, None),
        P(),
        P(("mic", "orient"), None),
        P(("mic", "orient"), None),
    )
    out_specs = (P("mic", None), P("mic", None), P("mic", None), P("mic", None))
    return jax.shard_map(body, mesh=mesh, in_specs=in_specs, out_specs=out_specs, check_vma=False)
```

```python
import functools
import math

import jax
import jax.numpy as jnp
import numpy as np
from jax import lax
from jax.experimental import pallas as pl
from jax.experimental.pallas import tpu as pltpu
from jax.sharding import PartitionSpec as P

MESH = pl.DeviceIdType.MESH
LOW = -3.0e38


def make_tables(box_edge):
    positions = np.arange(box_edge, dtype=np.int32)
    products = positions[:, None] * positions[None, :] % box_edge
    angles = products.astype(np.float32) * np.float32(2.0 * math.pi / box_edge)
    cosine = np.cos(angles)
    sines = np.sin(angles)
    narrow = lambda a: a.astype(np.float32).astype(jnp.bfloat16)
    fwd_cos, fwd_sin = narrow(cosine), narrow(sines)
    inv_cos = narrow(cosine / np.float32(box_edge))
    inv_sin = narrow(sines / np.float32(box_edge))
    return (fwd_cos, fwd_sin, inv_cos, inv_sin)


def forward(tile_image, fwd_cos, fwd_sin):
    box_edge = tile_image.shape[0]
    full_map = jnp.asarray(np.concatenate([fwd_cos, fwd_sin], 1))
    halved = jnp.dot(tile_image, full_map, preferred_element_type=jnp.float32).astype(jnp.bfloat16)
    ar, ai = halved[:, :box_edge], -halved[:, box_edge:]
    stacked = jnp.concatenate(
        [jnp.concatenate([ar, ai], 1), jnp.concatenate([ai, -ar], 1)], 0
    )
    return jnp.dot(full_map, stacked, preferred_element_type=jnp.float32).astype(jnp.bfloat16)


def fold_matrices(edge):
    half = edge // 2
    mirror = np.zeros((2 * edge, edge), np.float32)
    for l in range(1, half):
        mirror[edge - l, l] = 1.0
        mirror[2 * edge - l, half + l] = -1.0
    mirror[0, 0], mirror[edge + half, 0] = 0.5, 0.5
    mirror[edge, half], mirror[half, half] = -0.5, 0.5
    row = lax.broadcasted_iota(jnp.int32, (2 * edge, edge), 0)
    col = lax.broadcasted_iota(jnp.int32, (2 * edge, edge), 1)
    own = jnp.where(row == jnp.where(col < half, col, col + half), 1.0, 0.0)
    first = jnp.where(row == 0, 0.5, jnp.where(row == edge + half, -0.5, 0.0))
    middle = jnp.where((row == edge) | (row == half), 0.5, 0.0)
    own = jnp.where(col == 0, first, jnp.where(col == half, middle, own))
    return own.astype(jnp.bfloat16), jnp.asarray(mirror, jnp.bfloat16)


def fold_half(filtered):
    count, rows, width = filtered.shape
    edge = width // 2
    mics = lax.axis_size("mic")
    own_map, mirror_map = fold_matrices(edge)
    mirrored = jnp.einsum(
        "tkc,cl->tkl", filtered, mirror_map, preferred_element_type=jnp.float32
    ).astype(jnp.bfloat16)
    flip = np.zeros((rows, rows), np.float32)
    for i in range(1, rows):
        flip[i, rows - i] = 1.0
    turned = jnp.einsum(
        "ik,tkl->til", jnp.asarray(flip, jnp.bfloat16), mirrored, preferred_element_type=jnp.float32
    ).astype(jnp.bfloat16)
    first = lax.ppermute(mirrored[:, 0, :], "mic", [(m, (mics - m) % mics) for m in range(mics)])
    rest = lax.ppermute(turned, "mic", [(m, mics - 1 - m) for m in range(mics)])
    own = jnp.einsum("tkc,cl->tkl", filtered, own_map, preferred_element_type=jnp.float32)
    row = lax.broadcasted_iota(jnp.int32, (1, rows, 1), 1)
    other = jnp.where(row == 0, first[:, None, :].astype(jnp.float32), rest.astype(jnp.float32))
    return (own + other).astype(jnp.bfloat16)


def correlate(e, gr_ref, gi_ref, gb_ref, cs_ref, col_ref, flip_ref):
    edge = gr_ref.shape[0]
    half = edge // 2
    es = jnp.concatenate([e[:, half:], e[:, :half]], axis=1)
    gr = gr_ref[...]
    gi = gi_ref[...]
    lane = lax.broadcasted_iota(jnp.int32, (edge, edge), 1)
    low = lane < half
    narrow = lax.broadcasted_iota(jnp.int32, (edge, 128), 1)
    dr = jnp.dot(
        flip_ref[...],
        jnp.where(narrow == 0, e[:, :128], pltpu.roll(es[:, :128], 1, 1)).astype(jnp.bfloat16),
        preferred_element_type=jnp.float32,
    )
    gbr, gbi = gb_ref[:, 0:1], gb_ref[:, 1:2]
    mr, mi = dr[:, 0:1], dr[:, 1:2]
    fix_r = gbr * mr - gbi * mi
    fix_i = gbr * mi + gbi * mr
    ge, ges = gr * e, gr * es
    he, hes = gi * e, gi * es
    top = jnp.where(low, ge, -ge) + hes
    bottom = ges + jnp.where(low, -he, he)
    at_r, at_i = lane == 0, lane == half
    top = top + jnp.where(at_r, fix_r, jnp.where(at_i, fix_i, 0.0))
    bottom = bottom + jnp.where(at_r, -fix_i, jnp.where(at_i, fix_r, 0.0))
    stacked = jnp.concatenate([top.astype(jnp.bfloat16), bottom.astype(jnp.bfloat16)], axis=0)
    v = jnp.dot(cs_ref[...], stacked, preferred_element_type=jnp.float32).astype(jnp.bfloat16)
    return jnp.dot(v, col_ref[...], preferred_element_type=jnp.float32)


def accumulate(corr, peak_ref, total_ref, square_ref):
    peak_ref[...] = jnp.maximum(peak_ref[...], corr)
    total_ref[...] += corr
    square_ref[...] += corr * corr


def clear(peak_ref, total_ref, square_ref):
    peak_ref[...] = jnp.full(peak_ref.shape, -3.0e38, jnp.float32)
    total_ref[...] = jnp.zeros(total_ref.shape, jnp.float32)
    square_ref[...] = jnp.zeros(square_ref.shape, jnp.float32)


def refine_correlation(template, ctf_ref, g_ref, cs_ref):
    edge = ctf_ref.shape[0]
    gain = ctf_ref[...]
    narrow = lambda a: a.astype(jnp.bfloat16)
    fr = narrow(template[:, :edge].astype(jnp.float32) * gain).astype(jnp.float32)
    fi = narrow(template[:, edge:].astype(jnp.float32) * gain).astype(jnp.float32)
    gr = g_ref[:, :edge].astype(jnp.float32)
    gi = g_ref[:, edge:].astype(jnp.float32)
    zr = narrow(gr * fr + gi * fi)
    zi = narrow(gi * fr - gr * fi)
    ci, si = cs_ref[:, :edge], cs_ref[:, edge:]
    dot = lambda a, b: jnp.dot(a, b, preferred_element_type=jnp.float32)
    ur = narrow(dot(ci, zr) - dot(si, zi))
    ui = narrow(dot(si, zr) + dot(ci, zi))
    return dot(ur, ci) - dot(ui, si)


def search_kernel(e_ref, *refs):
    @pl.when(pl.program_id(0) == 0)
    def _():
        clear(*refs[6:])

    edge = refs[0].shape[0]
    e = e_ref[...].reshape(edge, edge).astype(jnp.float32)
    accumulate(correlate(e, *refs[:6]), *refs[6:])


def all_maps(folded, gr, gi, gb, cs, col, library, ctf, spectrum, wanted):
    count, rows, edge = folded.shape
    place = lambda axis: lax.broadcasted_iota(jnp.int32, (edge, edge), axis)
    flip = ((place(0) + place(1)) % edge == 0).astype(jnp.bfloat16)
    whole = lambda a: pl.BlockSpec(a.shape, lambda t: (0, 0))
    out = jax.ShapeDtypeStruct((edge, edge), jnp.float32)
    cost = pl.CostEstimate(
        flops=count * 350000000, bytes_accessed=count * 600000, transcendentals=0
    )
    refined = refine_map(library, ctf, spectrum, cs, wanted)
    gathered = lax.all_gather(folded, "mic", axis=1, tiled=True)[None]
    maps = pl.pallas_call(
        search_kernel,
        grid=(count,),
        in_specs=[pl.BlockSpec((1, 1, edge, edge), lambda t: (0, t, 0, 0))]
        + [whole(a) for a in (gr, gi, gb, cs, col, flip)],
        out_specs=[pl.BlockSpec((edge, edge), lambda t: (0, 0))] * 3,
        out_shape=[out] * 3,
        compiler_params=pltpu.CompilerParams(vmem_limit_bytes=40 * 1024 * 1024),
        cost_estimate=cost,
    )(gathered, gr, gi, gb, cs, col, flip)
    return merge([*maps, refined])


def refine_kernel(lib_ref, ctf_ref, g_ref, cs_ref, wanted_ref, out_ref):
    step = pl.program_id(0)
    edge = ctf_ref.shape[0]

    @pl.when(step == 0)
    def _():
        out_ref[...] = jnp.full((edge, edge), -3.0e38, jnp.float32)

    @pl.when(wanted_ref[step] > 0)
    def _():
        corr = refine_correlation(lib_ref[0], ctf_ref, g_ref, cs_ref)
        out_ref[...] = jnp.maximum(out_ref[...], corr)


def refine_map(library, ctf, spectrum, cs, wanted):
    count, edge, width = library.shape
    whole = lambda a: pl.BlockSpec(a.shape, lambda t: (0, 0))
    return pl.pallas_call(
        refine_kernel,
        grid=(count,),
        in_specs=[pl.BlockSpec((1, edge, width), lambda t: (t, 0, 0))]
        + [whole(a) for a in (ctf, spectrum, cs)]
        + [pl.BlockSpec(memory_space=pltpu.SMEM)],
        out_specs=pl.BlockSpec((edge, edge), lambda t: (0, 0)),
        out_shape=jax.ShapeDtypeStruct((edge, edge), jnp.float32),
        compiler_params=pltpu.CompilerParams(vmem_limit_bytes=40 * 1024 * 1024),
        cost_estimate=pl.CostEstimate(flops=count * 700000000, bytes_accessed=count * 1200000, transcendentals=0),
    )(library, ctf, spectrum, cs, wanted)


def join(left, right):
    right = [a.astype(jnp.float32) for a in right]
    return [
        jnp.maximum(a, b) if i in (0, 3) else a + b for i, (a, b) in enumerate(zip(left, right))
    ]


def merge(maps):
    size = lax.axis_size("orient")
    edge = maps[0].shape[0]
    half = edge // 2
    core = lax.axis_index("orient") % 2
    near = [(i, i ^ 1) for i in range(size)]
    narrow = lambda values: [a.astype(jnp.bfloat16) for a in values]
    mine = [lax.dynamic_slice_in_dim(a, core * half, half, 0) for a in maps]
    theirs = narrow(lax.dynamic_slice_in_dim(a, (1 - core) * half, half, 0) for a in maps)
    state = join(mine, lax.ppermute(jnp.stack(theirs), "orient", near))
    distance = 2
    while distance < size:
        far = [(i, i ^ distance) for i in range(size)]
        state = join(state, lax.ppermute(jnp.stack(narrow(state)), "orient", far))
        distance *= 2
    final = jnp.stack(narrow(state))
    other = lax.ppermute(final, "orient", near)
    first = jnp.where(core == 0, final, other)
    second = jnp.where(core == 0, other, final)
    return [jnp.concatenate([first[i], second[i]], 0).astype(jnp.float32) for i in range(len(maps))]


def quartered(search, library, edge):
    sizes = (lax.axis_size("mic"), lax.axis_size("orient"))
    return sizes == (8, 4) and edge == 384 and search.shape[:2] == (16, 48)


def column_plan(edge):
    half, lanes = edge // 2, 128
    plan = [("re", l) for l in range(half)]
    plan += [("im", l) for l in range(lanes, half)]
    return plan + [("im", l) for l in range(lanes)]


def quarter_tables(edge):
    half, slab, lanes = edge // 2, edge // 4, 128
    fwd_cos, fwd_sin, inv_cos, inv_sin = make_tables(edge)
    plan = column_plan(edge)
    packed = plan.index(("im", 0))
    own = np.zeros((2 * edge, edge), np.float32)
    mirror = np.zeros((2 * edge, edge), np.float32)
    freq, sign = [], []
    col = np.zeros((edge, edge), np.float32)
    for place, (kind, l) in enumerate(plan):
        freq.append(half if place == packed else l)
        sign.append(-1.0 if kind == "im" and place != packed else 1.0)
        if kind == "re":
            col[place] = inv_cos[l]
        else:
            col[place] = inv_cos[half] if place == packed else -inv_sin[l].astype(np.float32)
        if l == 0:
            continue
        if kind == "re":
            own[l, place] = 1.0
            mirror[edge - l, place] = 1.0
        else:
            own[edge + l, place] = 1.0
            mirror[2 * edge - l, place] = -1.0
    own[0, 0], own[edge + half, 0] = 0.5, -0.5
    own[edge, packed], own[half, packed] = 0.5, 0.5
    mirror[0, 0], mirror[edge + half, 0] = 0.5, 0.5
    mirror[edge, packed], mirror[half, packed] = -0.5, 0.5
    order = np.concatenate([np.arange(s * slab, (s + 1) * slab) for s in (0, 3, 1, 2)])
    flips = np.zeros((2, half + 16, half), np.float32)
    for pair, moved in enumerate((slab, 0)):
        for u in range(half):
            flips[pair, half if u == moved else u, (half - u) % half] = 1.0
    turn = np.zeros((edge, edge), np.float32)
    for i, k in enumerate(order):
        turn[i, list(order).index((edge - k) % edge)] = 1.0
    low = lambda a: jnp.asarray(np.asarray(a, np.float32), jnp.bfloat16)
    side = lambda a, b: low(np.concatenate([np.asarray(a, np.float32), np.asarray(b, np.float32)], 1))
    return dict(
        cs=side(inv_cos, inv_sin),
        cs_turned=side(inv_cos[:, order], inv_sin[:, order]),
        col=low(col),
        fold=side(own, mirror),
        flips=low(flips),
        turn=low(turn),
        full=side(fwd_cos, fwd_sin),
        full_cols=side(fwd_cos[:, freq], fwd_sin[:, freq]),
        full_rows=side(fwd_cos[order], fwd_sin[order]),
        sign=jnp.asarray(np.tile(np.asarray(sign, np.float32)[None], (8, 1))),
    )


TABLES = ("cs", "cs_turned", "col", "fold", "flips", "turn", "full", "full_cols", "full_rows", "sign")


def dot(a, b):
    return jnp.dot(a, b, preferred_element_type=jnp.float32)


def spectrum_of(image, columns, rows):
    edge = image.shape[0]
    halved = dot(image, columns).astype(jnp.bfloat16)
    ar, ai = halved[:, :edge], -halved[:, edge:]
    stacked = jnp.concatenate(
        [jnp.concatenate([ar, ai], 1), jnp.concatenate([ai, -ar], 1)], 0
    )
    return dot(rows, stacked).astype(jnp.bfloat16)


def quarter_kernel(ids_in, image_in, search_in, library_in, ctf_in, *refs):
    inputs, refs = refs[: len(TABLES)], refs[len(TABLES) :]
    final, refined = refs[:2]
    tables, refs = refs[2 : 2 + len(TABLES)], refs[2 + len(TABLES) :]
    tab = dict(zip(TABLES, tables))
    (image, library, ctf, images, raw, folded, gains, pair_e, stack, maps, refmap,
     x_out, x_in, y_out, y_in, z_out, z_in, shared, mask_out, mask_in, cap, g_own,
     ids_ref, block_in, sums, sum_raw, sum_e) = refs[:27]
    (load_sem, raw_s, raw_r, ez_s, ez_r, ec_s, ec_r, im_s, im_r, mk_s, mk_r, sh_s, sh_r,
     x_s, x_r, y_s, y_r, z_s, z_r, ag_s, ag_r, co_s, co_r, su_s, su_r, sr_s, sr_r, sx_s, sx_r) = refs[27:]
    edge = ctf.shape[0]
    half, slab, rows = edge // 2, edge // 4, raw.shape[1] // 4
    depth = raw.shape[0]
    listed = library.shape[0]
    me, block = lax.axis_index("mic"), lax.axis_index("orient")
    z, x = me // 2, me % 2
    y, c = block // 2, block % 2
    zm, xm, ym, cm = 3 - z, 1 - x, 1 - y, 1 - c
    zn = z + 1 - 2 * (z % 2)
    upper = z // 2
    outer = (z + 1) % 4 // 2
    home = c == x
    away = c != x
    place = lambda z, x, y, c: {"mic": z * 2 + x, "orient": y * 2 + c}
    trio = [(z, xm), (zm, x), (zm, xm)]
    peers = [(y, cm), (ym, c), (ym, cm)]
    partners = [place(a, b, y, c) for a, b in trio] + [place(z, x, a, b) for a, b in peers]
    partners.append(place(zn, x, y, c))

    barrier = pltpu.get_barrier_semaphore()
    for partner in partners:
        pl.semaphore_signal(barrier, inc=1, device_id=partner, device_id_type=MESH)

    def spot(zz, xx):
        return pl.ds(pl.multiple_of(zz // 2 * slab + xx * rows, 16), rows)

    loads = [
        pltpu.make_async_copy(image_in, image, load_sem.at[0]),
        pltpu.make_async_copy(ctf_in, ctf, load_sem.at[1]),
    ]
    for i, (a, b) in enumerate(zip(inputs, tables)):
        loads.append(pltpu.make_async_copy(a, b, load_sem.at[2 + i]))
    count = len(loads)
    lib_loads = [
        pltpu.make_async_copy(library_in.at[j], library.at[j], load_sem.at[count + j])
        for j in range(listed)
    ]
    count += listed
    own_loads = [
        pltpu.make_async_copy(
            search_in.at[x * 2 * depth + upper * depth + j],
            raw.at[j, spot(z, x)],
            load_sem.at[count + j],
        )
        for j in range(depth)
    ]
    named = [pltpu.make_async_copy(ids_in, ids_ref, load_sem.at[count + depth])]
    block_load = pltpu.make_async_copy(search_in, block_in, load_sem.at[count + depth + 1])
    block_load.start()
    for load in named + loads + lib_loads + own_loads:
        load.start()
    for load in named:
        load.wait()

    row = lax.broadcasted_iota(jnp.int32, mask_out.shape, 0)
    mask = jnp.zeros(mask_out.shape, jnp.float32)
    for entry in range(ids_ref.shape[1]):
        mask = jnp.where(row == ids_ref[0, entry], 1.0, mask)
    mask_out[...] = mask

    def remote(src, dst, send, recv, target):
        return pltpu.make_async_remote_copy(
            src_ref=src, dst_ref=dst, send_sem=send, recv_sem=recv, device_id=target, device_id_type=MESH
        )

    def send_raw(q, j):
        zz, xx = trio[q]
        return remote(
            search_in.at[xx * 2 * depth + zz // 2 * depth + j],
            raw.at[j, spot(z, x)],
            raw_s.at[q, j],
            raw_r.at[q, j],
            place(zz, xx, y, c),
        )

    def take_raw(q, j):
        zz, xx = trio[q]
        spots = raw.at[j, spot(zz, xx)]
        return remote(spots, spots, raw_s.at[q, j], raw_r.at[q, j], place(zz, xx, y, c))

    beside, across = place(z, xm, y, c), place(zm, x, y, c)
    send_own = remote(image_in, images.at[0], im_s.at[0], im_r.at[0], beside)
    mine = pl.ds(pl.multiple_of(y * half, 16), half)
    theirs = pl.ds(pl.multiple_of(ym * half, 16), half)
    twin = place(z, x, ym, c)
    core = place(z, x, y, cm)
    send_far = remote(image_in.at[mine], images.at[1, mine], im_s.at[1], im_r.at[1], across)
    pass_far = remote(images.at[1, mine], images.at[1, mine], im_s.at[2], im_r.at[2], beside)
    pass_twin = remote(images.at[1, mine], images.at[1, mine], im_s.at[3], im_r.at[3], twin)
    take_twin = remote(images.at[1, theirs], images.at[1, theirs], im_s.at[3], im_r.at[3], twin)

    def send_mask(q):
        yy, cc = peers[q]
        part = mask_out.at[pl.ds(pl.multiple_of((yy * 2 + cc) * listed, 8), listed)]
        return remote(part, mask_in.at[q], mk_s.at[q], mk_r.at[q], place(z, x, yy, cc))

    part_c = pl.ds(pl.multiple_of(c * half, 16), half)
    part_o = pl.ds(pl.multiple_of(cm * half, 16), half)
    share_core = remote(shared.at[0], shared.at[1], sh_s.at[0], sh_r.at[0], core)
    share_twin = remote(shared.at[2, part_c], shared.at[3, part_c], sh_s.at[1], sh_r.at[1], twin)
    share_last = remote(refined.at[part_c], refined.at[part_c], sh_s.at[2], sh_r.at[2], core)
    take_last = remote(refined.at[part_o], refined.at[part_o], sh_s.at[2], sh_r.at[2], core)

    def send_sum(q):
        yy, cc = peers[q]
        return remote(sums.at[0], sums.at[q + 1], su_s.at[q], su_r.at[q], place(z, x, yy, cc))

    def sum_part(slot, zz, xx, target):
        rows_of = sum_raw.at[c, spot(zz, xx)]
        return remote(rows_of, rows_of, sr_s.at[slot], sr_r.at[slot], target)

    sum_core = remote(sum_raw.at[c], sum_raw.at[c], sx_s.at[0], sx_r.at[0], core)
    sum_core_take = remote(sum_raw.at[cm], sum_raw.at[cm], sx_s.at[0], sx_r.at[0], core)
    sum_give = remote(sum_e.at[outer], sum_e.at[outer], sx_s.at[1], sx_r.at[1], place(zn, x, y, c))
    sum_take = remote(sum_e.at[1 - outer], sum_e.at[1 - outer], sx_s.at[1], sx_r.at[1], place(zn, x, y, c))
    total_core = remote(final.at[2], final.at[2], co_s.at[4], co_r.at[4], core)

    def send_e(j):
        part = folded.at[c, j, outer]
        return remote(part, part, ez_s.at[j], ez_r.at[j], place(zn, x, y, c))

    def take_e(j):
        part = folded.at[c, j, 1 - outer]
        return remote(part, part, ez_s.at[j], ez_r.at[j], place(zn, x, y, c))

    def core_e(j, source, pair):
        part = folded.at[source, j, pair]
        slot = pair * depth + j
        return remote(part, part, ec_s.at[slot], ec_r.at[slot], place(z, x, y, cm))

    pl.semaphore_wait(barrier, len(partners))
    for q in range(3):
        send_mask(q).start()
    pl.when(home)(lambda: send_far.start())
    for q in (1, 2, 0):
        send_raw(q, 0).start()
    send_raw(1, 1).start()
    pl.when(home)(lambda: send_own.start())

    refmap[...] = jnp.full(refmap.shape, LOW, jnp.float32)
    for t in range(2):
        maps[t, 0] = jnp.full((edge, edge), LOW, jnp.float32)
        maps[t, 1] = jnp.zeros((edge, edge), jnp.float32)
    for load in loads:
        load.wait()
    block_load.wait()
    own_gain = ctf[pl.ds(pl.multiple_of(me * rows, 8), rows), :]
    own_gain = jnp.concatenate([own_gain, own_gain], 1)

    def add_one(t, acc):
        scaled = (block_in[t].astype(jnp.float32) * own_gain).astype(jnp.bfloat16)
        return acc + scaled.astype(jnp.float32)

    acc = lax.fori_loop(0, block_in.shape[0], add_one, jnp.zeros(own_gain.shape, jnp.float32))
    sums[0] = acc.astype(jnp.bfloat16)
    for q in range(3):
        send_sum(q).start()
    g_own[...] = spectrum_of(image[...], tab["full"][...], tab["full"][...])
    wanted = mask_out[pl.ds(pl.multiple_of(block * listed, 8), listed), :]
    for q in range(3):
        send_mask(q).wait_recv()
        wanted = jnp.maximum(wanted, mask_in[q])
    cap[...] = jnp.where(wanted > 0.0, -LOW, LOW)
    for load in lib_loads:
        load.wait()

    def refine_some(first, last):
        def one(j, carry):
            corr = refine_correlation(library[j], ctf, g_own, tab["cs"])
            refmap[...] = jnp.maximum(refmap[...], jnp.minimum(corr, cap[pl.ds(j, 1), :]))
            return carry

        lax.fori_loop(first, last, one, 0)

    def gain_of(t, picture):
        spec = spectrum_of(picture, tab["full_cols"][...], tab["full_rows"][...]).astype(jnp.float32)
        gr, gi, sign = spec[:, :edge], spec[:, edge:], tab["sign"][0:1, :]
        gains[t, 0] = gr * sign
        gains[t, 1] = gi
        gains[t, 2] = gr
        gains[t, 3] = -gi * sign

    def fold_into(target, filtered):
        both = dot(filtered, tab["fold"][...])
        turned = dot(tab["flips"][outer], both[:, edge:].astype(jnp.bfloat16))
        target[0:half, :] = (both[:, :edge] + turned[0:half]).astype(jnp.bfloat16)
        target[half : half + 16, :] = turned[half:].astype(jnp.bfloat16)

    def fold(j):
        for q in range(3):
            take_raw(q, j).wait_recv()
        own_loads[j].wait()
        near = ctf[pl.ds(pl.multiple_of(outer * slab, 8), slab), :]
        far = ctf[pl.ds(pl.multiple_of((3 - outer) * slab, 8), slab), :]
        gain = jnp.concatenate([near, far], 0)
        gain = jnp.concatenate([gain, gain], 1)
        filtered = (raw[j].astype(jnp.float32) * gain).astype(jnp.bfloat16)
        fold_into(folded.at[c, j, outer], filtered)
        send_e(j).start()
        if j + 2 < depth:
            for q in (1, 2, 0):
                send_raw(q, j).wait_send()
                send_raw(q, j + 2).start()
        core_e(j, c, outer).start()

    def prepare_one(source, held):
        parts = [held[p].astype(jnp.float32) for p in range(2)]
        e = jnp.concatenate(
            [
                parts[0][0:slab],
                parts[0][slab : slab + 16] + parts[1][half:],
                parts[0][slab + 16 : half],
                parts[1][0:16] + parts[0][half:],
                parts[1][16:half],
            ],
            0,
        )
        t0, t1, t2 = e[:, 0:128], e[:, 128:256], e[:, 256:384]
        back = dot(tab["turn"][...], jnp.concatenate([t0, t2], 1).astype(jnp.bfloat16))
        m0, m2 = back[:, 0:128], back[:, 128:256]
        first = lax.broadcasted_iota(jnp.int32, t0.shape, 1) == 0
        pair_e[source, 0, :, 0:128] = jnp.where(first, 0.5 * (t0 + m0), t0)
        pair_e[source, 0, :, 128:256] = t1
        pair_e[source, 0, :, 256:384] = jnp.where(first, 0.5 * (t2 + m2), t2)
        pair_e[source, 1, :, 0:128] = jnp.where(first, 0.5 * (t2 - m2), t2)
        pair_e[source, 1, :, 128:256] = pltpu.roll(t1, 64, 1)
        pair_e[source, 1, :, 256:384] = jnp.where(first, 0.5 * (m0 - t0), t0)

    def prepare(j):
        prepare_one(0, folded.at[0, j])
        prepare_one(1, folded.at[1, j])

    def search(t):
        for n in range(2):
            e, es = pair_e[n, 0], pair_e[n, 1]
            stack[0:edge, n * edge : (n + 1) * edge] = (gains[t, 0] * e + gains[t, 1] * es).astype(jnp.bfloat16)
            stack[edge:, n * edge : (n + 1) * edge] = (gains[t, 2] * es + gains[t, 3] * e).astype(jnp.bfloat16)
        v = dot(tab["cs_turned"][...], stack[...]).astype(jnp.bfloat16)
        one = dot(v[:, 0:edge], tab["col"][...])
        two = dot(v[:, edge:], tab["col"][...])
        maps[t, 0] = jnp.maximum(maps[t, 0], jnp.maximum(one, two))
        maps[t, 1] += one * one + two * two

    def total_map():
        prepare_one(0, sum_e)
        e, es = pair_e[0, 0], pair_e[0, 1]
        stack[0:edge, 0:edge] = (gains[0, 0] * e + gains[0, 1] * es).astype(jnp.bfloat16)
        stack[edge:, 0:edge] = (gains[0, 2] * es + gains[0, 3] * e).astype(jnp.bfloat16)
        v = dot(tab["cs_turned"][...], stack[:, 0:edge]).astype(jnp.bfloat16)
        final[2] = dot(v, tab["col"][...]).astype(jnp.bfloat16)

    def await_core(j):
        core_e(j, cm, outer).wait_recv()
        core_e(j, cm, 1 - outer).wait_recv()

    def templates(j):
        await_core(j)
        prepare(j)

        def one(t, carry):
            search(t)
            return carry

        lax.fori_loop(0, 2, one, 0)

    def arrive(j):
        take_e(j).wait_recv()
        core_e(j, c, 1 - outer).start()

    eighth = lambda n: listed * n // 8
    refine_some(0, eighth(1))

    @pl.when(home)
    def _():
        send_far.wait_recv()
        pass_far.start()
        pass_twin.start()
        images[0] = image[...]

    acc = sums[0].astype(jnp.float32)
    for q in range(3):
        send_sum(q).wait_recv()
        acc = acc + sums[q + 1].astype(jnp.float32)
    sum_raw[c, spot(z, x)] = jnp.where(c == 0, acc[:, :edge], acc[:, edge:]).astype(jnp.bfloat16)
    sum_part(1, z, x, across).start()
    sum_part(0, z, x, beside).start()
    for q in (2, 0):
        send_raw(q, 1).start()
    refine_some(eighth(1), eighth(3))
    fold(0)
    sum_part(1, zm, x, across).wait_recv()
    sum_part(2, zm, x, beside).start()

    @pl.when(away)
    def _():
        pass_far.wait_recv()
        pass_twin.start()
        send_own.wait_recv()

    gain_of(0, images[0])
    refine_some(eighth(3), eighth(5))
    fold(1)
    arrive(0)
    take_twin.wait_recv()
    gain_of(1, images[1])
    templates(0)
    sum_part(0, z, xm, beside).wait_recv()
    sum_part(2, zm, xm, beside).wait_recv()

    @pl.when(away)
    def _():
        sum_core.start()

    arrive(1)
    fold(2)

    @pl.when(home)
    def _():
        sum_core_take.wait_recv()
        fold_into(sum_e.at[outer], jnp.concatenate([sum_raw[0], sum_raw[1]], 1))
        sum_give.start()

    templates(1)
    refine_some(eighth(5), listed)
    shared[0] = refmap[...].astype(jnp.bfloat16)
    share_core.start()
    fold(3)
    arrive(2)

    @pl.when(home)
    def _():
        sum_take.wait_recv()
        total_map()
        total_core.start()

    share_core.wait_recv()
    shared[2] = jnp.maximum(shared[0], shared[1])
    share_twin.start()
    templates(2)
    arrive(3)
    share_twin.wait_recv()
    refined[part_c] = jnp.maximum(shared[2, part_c], shared[3, part_c])
    share_last.start()
    await_core(3)
    prepare(3)

    quarter = half // 2
    keep = [pl.ds(pl.multiple_of(a * half + y * quarter, 16), quarter) for a in range(2)]
    give = [pl.ds(pl.multiple_of(a * half + ym * quarter, 16), quarter) for a in range(2)]
    upper_rows = slice(0, half)

    def x_send(t, part):
        rows = pl.ds(0, half) if part == 0 else keep[1]
        return remote(x_out.at[t, :, rows], x_in.at[t, :, rows], x_s.at[t, part], x_r.at[t, part], beside)

    def y_send(t, part):
        return remote(y_out.at[t, part], y_in.at[t, part], y_s.at[t, part], y_r.at[t, part], twin)

    def z_send(part):
        return remote(z_out.at[part], z_in.at[part], z_s.at[part], z_r.at[part], across)

    def final_send(part):
        return remote(final.at[0:2, keep[part]], final.at[0:2, keep[part]], ag_s.at[part], ag_r.at[part], twin)

    def final_take(part):
        return remote(final.at[0:2, give[part]], final.at[0:2, give[part]], ag_s.at[part], ag_r.at[part], twin)

    def core_final(part, where):
        rows = (keep, give)[where][part]
        slot = where * 2 + part
        return remote(final.at[0:2, rows], final.at[0:2, rows], co_s.at[slot], co_r.at[slot], core)

    def merge_in(t, where, piece):
        maps[t, 0, where] = jnp.maximum(maps[t, 0, where], piece[0].astype(jnp.float32))
        maps[t, 1, where] += piece[1].astype(jnp.float32)

    def start_y(t, part):
        y_out[t, part] = maps[t, :, give[part]].astype(jnp.bfloat16)
        y_send(t, part).start()

    def start_x(t, part):
        rows = upper_rows if part == 0 else keep[1]
        x_out[t, :, rows] = maps[t, :, rows].astype(jnp.bfloat16)
        x_send(t, part).start()

    def start_z(part):
        z_out[part] = maps[1, :, keep[part]].astype(jnp.bfloat16)
        z_send(part).start()

    def relay(t):
        x_send(t, 0).wait_recv()
        merge_in(t, give[0], x_in[t, :, give[0]])
        start_y(t, 0)
        merge_in(t, keep[0], x_in[t, :, keep[0]])

    search(1)
    pl.when(away)(lambda: start_x(1, 0))
    start_y(1, 1)
    search(0)
    pl.when(home)(lambda: relay(1))
    y_send(1, 1).wait_recv()
    merge_in(1, keep[1], y_in[1, 1])

    @pl.when(away)
    def _():
        start_x(1, 1)
        start_x(0, 0)

    start_y(0, 1)

    @pl.when(home)
    def _():
        y_send(1, 0).wait_recv()
        merge_in(1, keep[0], y_in[1, 0])
        start_z(0)
        x_send(1, 1).wait_recv()
        merge_in(1, keep[1], x_in[1, :, keep[1]])
        start_z(1)
        relay(0)

    y_send(0, 1).wait_recv()
    merge_in(0, keep[1], y_in[0, 1])
    pl.when(away)(lambda: start_x(0, 1))

    @pl.when(home)
    def _():
        y_send(0, 0).wait_recv()
        merge_in(0, keep[0], y_in[0, 0])
        x_send(0, 1).wait_recv()
        merge_in(0, keep[1], x_in[0, :, keep[1]])

    @pl.when(home)
    def _():
        for part in range(2):
            z_send(part).wait_recv()
            merge_in(0, keep[part], z_in[part])
            final[0:2, keep[part]] = maps[0, :, keep[part]].astype(jnp.bfloat16)
            final_send(part).start()
            core_final(part, 0).start()
        for part in range(2):
            final_take(part).wait_recv()
            core_final(part, 1).start()
        for part in range(2):
            y_send(0, part).wait_send()
            y_send(1, part).wait_send()
            z_send(part).wait_send()
            final_send(part).wait_send()
            core_final(part, 0).wait_send()
            core_final(part, 1).wait_send()

    @pl.when(away)
    def _():
        sum_core.wait_send()
        total_core.wait_recv()
        for part in range(2):
            x_send(0, part).wait_send()
            x_send(1, part).wait_send()
            y_send(part, 1).wait_send()
        for part in range(2):
            core_final(part, 0).wait_recv()
        for part in range(2):
            core_final(part, 1).wait_recv()

    take_last.wait_recv()
    share_core.wait_send()
    share_twin.wait_send()
    share_last.wait_send()
    pass_twin.wait_send()
    for q in range(3):
        send_mask(q).wait_send()
        send_sum(q).wait_send()
    sum_part(0, z, x, beside).wait_send()
    sum_part(1, z, x, across).wait_send()
    sum_part(2, zm, x, beside).wait_send()
    for j in range(depth):
        for q in range(3):
            if j + 2 >= depth:
                send_raw(q, j).wait_send()
        send_e(j).wait_send()
        core_e(j, c, outer).wait_send()
        core_e(j, c, 1 - outer).wait_send()

    @pl.when(home)
    def _():
        sum_give.wait_send()
        total_core.wait_send()
        send_own.wait_send()
        send_far.wait_send()
        pass_far.wait_send()


def finish_kernel(number, final, best, peak, mean, scaled, refined):
    top = final[0].astype(jnp.float32)
    peak[...] = top
    mean[...] = final[2].astype(jnp.float32) / number
    scaled[...] = top * lax.rsqrt(final[1].astype(jnp.float32) / number + 1e-05)
    refined[...] = best[...].astype(jnp.float32)


def quarter_maps(micrograph, search, library, ctf, ref_owner, ref_slot):
    edge = micrograph.shape[1]
    half, depth, listed = edge // 2, search.shape[0] // 4, library.shape[0]
    ids = (ref_owner * listed + ref_slot).reshape(1, -1)
    tables = quarter_tables(edge)
    given = [tables[name] for name in TABLES]
    any_space = pl.BlockSpec(memory_space=pl.ANY)
    vmem = pl.BlockSpec(memory_space=pltpu.VMEM)
    low, wide = jnp.bfloat16, jnp.float32
    dma = lambda *shape: pltpu.SemaphoreType.DMA(shape)
    scratch = [pltpu.VMEM(a.shape, a.dtype) for a in given]
    scratch += [
        pltpu.VMEM((edge, edge), low),
        pltpu.VMEM(library.shape, low),
        pltpu.VMEM((edge, edge), wide),
        pltpu.VMEM((2, edge, edge), low),
        pltpu.VMEM((depth, half, 2 * edge), low),
        pltpu.VMEM((2, depth, 2, half + 16, edge), low),
        pltpu.VMEM((2, 4, edge, edge), wide),
        pltpu.VMEM((2, 2, edge, edge), wide),
        pltpu.VMEM((2 * edge, 2 * edge), low),
        pltpu.VMEM((2, 2, edge, edge), wide),
        pltpu.VMEM((edge, edge), wide),
        pltpu.VMEM((2, 2, edge, edge), low),
        pltpu.VMEM((2, 2, edge, edge), low),
        pltpu.VMEM((2, 2, 2, half // 2, edge), low),
        pltpu.VMEM((2, 2, 2, half // 2, edge), low),
        pltpu.VMEM((2, 2, half // 2, edge), low),
        pltpu.VMEM((2, 2, half // 2, edge), low),
        pltpu.VMEM((4, edge, edge), low),
        pltpu.VMEM((4 * listed, edge), wide),
        pltpu.VMEM((3, listed, edge), wide),
        pltpu.VMEM((listed, edge), wide),
        pltpu.VMEM((edge, 2 * edge), low),
        pltpu.SMEM(ids.shape, jnp.int32),
        pltpu.VMEM(search.shape, low),
        pltpu.VMEM((4,) + search.shape[1:], low),
        pltpu.VMEM((2, half, edge), low),
        pltpu.VMEM((2, half + 16, edge), low),
        dma(2 + len(given) + listed + depth + 2),
        dma(3, depth),
        dma(3, depth),
        dma(depth),
        dma(depth),
        dma(2 * depth),
        dma(2 * depth),
        dma(4),
        dma(4),
        dma(3),
        dma(3),
        dma(3),
        dma(3),
        dma(2, 2),
        dma(2, 2),
        dma(2, 2),
        dma(2, 2),
        dma(2),
        dma(2),
        dma(2),
        dma(2),
        dma(5),
        dma(5),
        dma(3),
        dma(3),
        dma(3),
        dma(3),
        dma(2),
        dma(2),
    ]
    final, refined = pl.pallas_call(
        quarter_kernel,
        in_specs=[any_space] * (5 + len(given)),
        out_specs=[vmem, vmem],
        out_shape=[
            jax.ShapeDtypeStruct((3, edge, edge), low),
            jax.ShapeDtypeStruct((edge, edge), low),
        ],
        scratch_shapes=scratch,
        compiler_params=pltpu.CompilerParams(
            vmem_limit_bytes=60 * 1024 * 1024, collective_id=0, has_side_effects=True
        ),
        cost_estimate=pl.CostEstimate(flops=12000000000, bytes_accessed=12000000, transcendentals=0),
    )(ids, micrograph, search, library, ctf, *given)
    number = float(lax.axis_size("orient") * search.shape[0])
    block = lambda: pl.BlockSpec((edge, edge), lambda i: (0, 0))
    return tuple(
        pl.pallas_call(
            functools.partial(finish_kernel, number),
            grid=(1,),
            in_specs=[vmem, vmem],
            out_specs=[block()] * 4,
            out_shape=[jax.ShapeDtypeStruct((edge, edge), wide)] * 4,
        )(final, refined)
    )


def body(micrograph, search_spectra, refine_spectra, ctf, ref_owner, ref_slot):
    edge = micrograph.shape[1]
    if quartered(search_spectra, refine_spectra, edge):
        return quarter_maps(micrograph, search_spectra, refine_spectra[0], ctf, ref_owner, ref_slot)
    half = edge // 2
    fwd_cos, fwd_sin, inv_cos, inv_sin = make_tables(edge)
    ctf_gain = jnp.concatenate([ctf, ctf], 1)
    rows_owned = search_spectra.shape[1]
    first_row = lax.axis_index("mic") * rows_owned
    own_gain = lax.dynamic_slice_in_dim(ctf_gain, first_row, rows_owned, 0)
    filtered = (search_spectra.astype(jnp.float32) * own_gain).astype(jnp.bfloat16)
    folded = fold_half(filtered)
    spectrum = forward(micrograph, fwd_cos, fwd_sin)

    library = refine_spectra[0]
    block_size = library.shape[0]
    ids = lax.all_gather(ref_owner[:, 0] * block_size + ref_slot[:, 0], "orient", axis=0, tiled=True)
    slots = lax.axis_index("orient") * block_size + jnp.arange(block_size, dtype=jnp.int32)
    wanted = jnp.any(slots[:, None] == ids[None, :], axis=1).astype(jnp.int32)
    cs = jnp.asarray(np.concatenate([inv_cos, inv_sin], 1))

    spec = spectrum.astype(jnp.float32)
    g_r, g_i = spec[:, :edge], spec[:, edge:]
    dc = jnp.stack([g_r[:, 0], g_i[:, 0]], 1)
    ny = jnp.stack([g_r[:, half], g_i[:, half]], 1)
    ga = (dc - ny) * 0.5
    gb = (dc + ny) * 0.5
    lane = lax.broadcasted_iota(jnp.int32, (edge, half), 1)
    h_r = jnp.where(lane == 0, ga[:, 0:1], g_r[:, :half])
    h_i = jnp.where(lane == 0, ga[:, 1:2], g_i[:, :half])
    gr = jnp.concatenate([h_r, h_r], 1)
    gi = jnp.concatenate([h_i, h_i], 1)
    sin_rows = -inv_sin[:half]
    sin_rows[0] = inv_cos[half]
    col = jnp.asarray(np.concatenate([inv_cos[:half], sin_rows], 0))
    peak, total, square, refined = all_maps(
        folded, gr, gi, gb, cs, col, library, ctf, spectrum, wanted
    )
    count = float(lax.axis_size("orient") * search_spectra.shape[0])
    return (peak, total / count, peak * lax.rsqrt(square / count + 1e-05), refined)


def solution(mesh):
    in_specs = (
        P("mic", None),
        P("orient", "mic", None),
        P("mic", "orient", None, None),
        P(),
        P(("mic", "orient"), None),
        P(("mic", "orient"), None),
    )
    out_specs = (P("mic", None), P("mic", None), P("mic", None), P("mic", None))
    return jax.shard_map(body, mesh=mesh, in_specs=in_specs, out_specs=out_specs, check_vma=False)
```
